256 devices in a mesh: band: 8 (over y, core), slab: 32 (over z, x).
Axes of the slice: x: 4, y: 4, z: 8, core: 2. Of those that a mesh axis runs over, the one named last changes fastest.
Arguments:
- bands: float32 [2, 256, 131072], P(None, ('band', 'slab')), may hold values from -6 to 6
- projectors: float32 [16384, 512], P('slab'), may hold values from -0.625 to 0.625
- slot_atom: int32 [16384], P('slab'), may hold values from -1 to 3071, as said below
- slot_box: int32 [16384], P('slab'), may hold values from 0 to 63
- channels: int32 [3072], replicated, may hold values from 1 to 8
- coupling: float32 [8, 8, 3072], replicated, may hold values from -2 to 2
Outputs:
- applied: float32 [2, 256, 131072], P(None, ('band', 'slab'))
The draws below stay inside these ranges and needn't reach their ends.
Inputs may be any that keep to these rules, and one draw needn't show every extreme that they name: `slot_atom`: atom a is owned by slab a // 96. A live slot k names an atom owned by slab k // 512 or by the slab before it, cyclically. In each slab's 512 slots the live ones come first; some slab has all of its slots live.
All inputs are finite; a program needn't handle non-finite values.
Results may differ from the reference program's by a relative error of at most 0.0003.
Values sent between devices are 32-bit elements; how exact they have to be, the bound alone decides.
A program may use at most 128 MiB of HBM per device.

```python
import jax
import jax.numpy as jnp
from jax import lax

NBLOCK = 2
BANDS = 256
CH = 8
BOXPTS = 64
BOX_DEV = 64
ATOM_DEV = 96
BLK_DEV = 512
NBLK = 16384
NATOM = 3072
NGRID = 131072
N_SLAB = 32


def slot_tables(key):
    slabs = NBLK // BLK_DEV
    keys = jax.random.split(key, 6)
    full = jax.random.randint(keys[0], (), 0, slabs)
    lowest = BLK_DEV // 8
    spread = BLK_DEV - lowest
    first_draw = jax.random.randint(keys[1], (slabs,), 0, spread + 1)
    second_draw = jax.random.randint(keys[2], (slabs,), 0, spread + 1)
    live_count = lowest + first_draw * second_draw // spread
    slab_ids = jnp.arange(slabs, dtype=jnp.int32)
    live_count = jnp.where(slab_ids == full, BLK_DEV, live_count)
    live_count = jnp.where(slab_ids == (full + 1) % slabs, lowest, live_count)
    slot = jnp.arange(NBLK, dtype=jnp.int32)
    slab_of = slot // BLK_DEV
    position = slot % BLK_DEV
    backward = jax.random.randint(keys[3], (NBLK,), 0, 2)
    within = jax.random.randint(keys[4], (NBLK,), 0, ATOM_DEV)
    atom = (slab_of - backward) % slabs * ATOM_DEV + within
    boxes = jax.random.randint(keys[5], (NBLK,), 0, BOX_DEV)
    marked = slot == NBLK - BLK_DEV
    atom = jnp.where(marked, NATOM - 1, atom)
    boxes = jnp.where(marked, BOX_DEV - 1, boxes)
    live = position < live_count[slab_of]
    atom = jnp.where(live, atom, -1)
    return (atom.astype(jnp.int32), boxes.astype(jnp.int32))


def draw_slot_atom(key, part):
    return slot_tables(jax.random.fold_in(key, 7))[0]


def draw_slot_box(key, part):
    return slot_tables(jax.random.fold_in(key, 7))[1]


def touch_ends(drawn, key, smallest, high):
    index_at = [jax.random.randint(jax.random.fold_in(key, axis), (), 0, length) for axis, length in enumerate(drawn.shape)]
    longest = drawn.shape.index(max(drawn.shape))
    beside = index_at[:longest] + [(index_at[longest] + 1) % drawn.shape[longest]] + index_at[longest + 1:]
    return drawn.at[tuple(index_at)].set(smallest).at[tuple(beside)].set(high)


def shard_levels(rng, shape, cuts, least, high):
    def one(dim, parts):
        heights = jax.random.uniform(jax.random.fold_in(jax.random.fold_in(rng, 6), dim), (parts,), jnp.float32, least / len(cuts), high / len(cuts))
        return jnp.repeat(jnp.exp(heights), shape[dim] // parts).reshape((-1,) + (1,) * (len(shape) - dim - 1))

    loudness = one(*cuts[0])
    for cut in cuts[1:]:
        loudness = loudness * one(*cut)
    return loudness


def gaussian(own_key, dims, deviation, most, cuts=(), kind=jnp.bfloat16):
    level = shard_levels(own_key, dims, cuts, -0.22, 0.18) if cuts else 1.0
    values = jax.random.normal(own_key, dims, jnp.float32) * deviation * level
    return jnp.minimum(jnp.maximum(values, -most), most).astype(kind)


def setup_inputs(seed: int = 0) -> dict:
    key_list = jax.random.split(jax.random.key(seed), 7)
    return {
        "bands": gaussian(key_list[0], (NBLOCK, BANDS, NGRID), 1.0, 6.0, ((1, 256),), jnp.float32),
        "projectors": gaussian(key_list[1], (NBLK, CH * BOXPTS), 0.1, 0.625, ((0, 32),), jnp.float32),
        "slot_atom": draw_slot_atom(jax.random.fold_in(key_list[6], 71), 0),
        "slot_box": draw_slot_box(jax.random.fold_in(key_list[6], 71), 0),
        "channels": touch_ends(jax.random.randint(key_list[4], (NATOM,), 1, CH + 1), jax.random.fold_in(key_list[4], 1), 1, CH).astype(jnp.int32),
        "coupling": gaussian(key_list[5], (CH, CH, NATOM), 0.35, 2.0, (), jnp.float32),
    }


def reference(bands, projectors, slot_atom, slot_box, channels, coupling):
    nblock, nband, ngrid = bands.shape
    highest = lax.Precision.HIGHEST
    slab_bands = bands.reshape(nblock, nband, N_SLAB, BOX_DEV, BOXPTS).transpose(2, 0, 1, 3, 4)
    beta_all = projectors.reshape(N_SLAB, BLK_DEV, CH, BOXPTS)
    atoms_all = slot_atom.reshape(N_SLAB, BLK_DEV)
    boxes_all = slot_box.reshape(N_SLAB, BLK_DEV).astype(jnp.int32)

    def project(carry, inputs):
        slab, beta, atoms, boxes = inputs
        live = (atoms >= 0).astype(slab.dtype)
        safe = jnp.where(atoms >= 0, atoms, 0).astype(jnp.int32)
        patches = jnp.take(slab, boxes, axis=2)
        term = jnp.einsum('nbkg,kcg->kncb', patches, beta, precision=highest)
        term = term * live[:, None, None, None]
        return carry + jax.ops.segment_sum(term, safe, num_segments=NATOM), None

    start = jnp.zeros((NATOM, nblock, CH, nband), bands.dtype)
    proj, _ = lax.scan(project, start, (slab_bands, beta_all, atoms_all, boxes_all))
    mask = (jnp.arange(CH, dtype=jnp.int32)[None, :] < channels[:, None]).astype(bands.dtype)
    masked = proj * mask[:, None, :, None]
    coef = jnp.einsum('cea,aneb->ancb', coupling, masked, precision=highest) * mask[:, None, :, None]

    def apply(inputs):
        beta, atoms, boxes = inputs
        live = (atoms >= 0).astype(bands.dtype)
        safe = jnp.where(atoms >= 0, atoms, 0).astype(jnp.int32)
        per_slot = jnp.take(coef, safe, axis=0) * live[:, None, None, None]
        contrib = jnp.einsum('kncb,kcg->nbkg', per_slot, beta, precision=highest)
        out = jnp.zeros((nblock, nband, BOX_DEV, BOXPTS), bands.dtype)
        return out.at[:, :, boxes, :].add(contrib)

    slabs_out = lax.map(apply, (beta_all, atoms_all, boxes_all))
    return slabs_out.transpose(1, 2, 0, 3, 4).reshape(nblock, nband, ngrid)
```

```python
import jax
import jax.numpy as jnp
from jax import lax
from jax.experimental import pallas as pl
from jax.experimental.pallas import tpu as pltpu
from jax.sharding import PartitionSpec as P

MESH = pl.DeviceIdType.MESH
F32 = jnp.float32
BF16 = jnp.bfloat16
NSLAB = 32
PTS = 64
BOXES = 64
TILES = BOXES // 2
SLOTS = 512
HALF = SLOTS // 2
CH = 8
ATOMS = 96
NATOM = NSLAB * ATOMS
NB = 32
WIN = 256


def split(x):
    hi = x.astype(BF16)
    lo = (x - hi.astype(F32)).astype(BF16)
    return hi, lo


def mm(a, b):
    return jnp.dot(a, b, preferred_element_type=F32)


def mm_nt(a, b, precision=None):
    return lax.dot_general(
        a, b, (((1,), (1,)), ((), ())), preferred_element_type=F32, precision=precision
    )


def iota(shape, axis):
    return lax.broadcasted_iota(jnp.int32, shape, axis)


def prepare_slots(pj, lf, lhs, bw):
    for q in range(4):
        v = pj[:, 128 * q : 128 * (q + 1)]
        lf[pl.ds(2 * q, SLOTS, stride=CH), :] = v
        lf[pl.ds(2 * q + 1, SLOTS, stride=CH), :] = pltpu.roll(v, 64, 1)
    low = iota((128, 128), 1) < 64

    def one(i, carry):
        rows = pl.ds(pl.multiple_of(i * 128, 128), 128)
        x = lf[rows, :]
        both = jnp.where(low, x, pltpu.roll(x, 64, 1))
        hi = both.astype(BF16).astype(F32)
        lo = both - hi
        lhs[rows, 0:128] = hi.astype(BF16)
        lhs[rows, 128:256] = jnp.where(low, lo, 0.0).astype(BF16)
        lf[rows, :] = both
        return carry

    lax.fori_loop(0, SLOTS * CH // 128, one, 0)
    keep = (iota((16, 128), 0) < 8) == (iota((16, 128), 1) < 64)

    def two(g, carry):
        for i in range(8):
            first = pl.multiple_of((g * 8 + i) * CH, CH)
            second = pl.multiple_of((HALF + g * 8 + i) * CH, CH)
            x = jnp.concatenate([lf[pl.ds(first, CH), :], lf[pl.ds(second, CH), :]], axis=0)
            x = jnp.where(keep, x, 0.0)
            hi = x.astype(BF16)
            lo = (x - hi.astype(F32)).astype(BF16)
            bw[g, 16 * i : 16 * (i + 1), 0:128] = hi
            bw[g, 16 * i : 16 * (i + 1), 128:256] = lo
        return carry

    lax.fori_loop(0, HALF // 8, two, 0)


def prepare_tables(me, meta, cw, sel, b4, md, start):
    slot_atom = meta[0:1, 0:SLOTS]
    slot_box = meta[0:1, SLOTS : 2 * SLOTS]
    live = slot_atom >= 0
    prev_start = lax.rem(me + NSLAB - 1, NSLAB) * ATOMS
    rel = slot_atom - prev_start
    rel = jnp.where(rel < 0, rel + NATOM, rel)
    rel = jnp.where(live, rel, -1)
    sel[...] = jnp.where(iota((2 * ATOMS, SLOTS), 0) == rel, 1.0, 0.0).astype(BF16)
    box = jnp.where(live, slot_box, -1)
    row = iota((TILES, HALF), 0)
    for i2 in range(2):
        part = box[:, HALF * i2 : HALF * (i2 + 1)]
        for p in range(2):
            at = (2 * i2 + p) * TILES
            b4[at : at + TILES, :] = jnp.where(2 * row + p == part, 1.0, 0.0).astype(BF16)
    offset = me * ATOMS - start
    own = jnp.where(iota((ATOMS, WIN), 1) == iota((ATOMS, WIN), 0) + offset, 1.0, 0.0)
    mixing = mm_nt(own, cw[0:72, :], lax.Precision.HIGHEST)
    count = mixing[:, 64:65]
    pair_channel = iota((ATOMS, 64), 1)
    keep = (lax.div(pair_channel, CH).astype(F32) < count) & (
        lax.rem(pair_channel, CH).astype(F32) < count
    )
    mixing = jnp.where(keep, mixing[:, 0:64], 0.0)
    pair = iota((64, CH * NB), 0)
    to = lax.div(iota((64, CH * NB), 1), NB)
    for d in range(CH):
        source = lax.rem(to + CH - d, CH)
        spread = jnp.where(pair == to * CH + source, 1.0, 0.0)
        md[d] = jnp.dot(
            mixing, spread, preferred_element_type=F32, precision=lax.Precision.HIGHEST
        )


def split_bands(xb, xs):
    low = iota((NB, 128), 1) < 64

    def one(r, carry):
        x = xb[r]
        turned = pltpu.roll(x, 64, 1)
        for p in range(2):
            both = jnp.where(low, x, turned) if p == 0 else jnp.where(low, turned, x)
            hi = both.astype(BF16).astype(F32)
            lo = both - hi
            xs[2 * r + p, :, 0:128] = jnp.where(low, hi, lo).astype(BF16)
            xs[2 * r + p, :, 128:256] = hi.astype(BF16)
        return carry

    lax.fori_loop(0, TILES, one, 0, unroll=2)


def project(slot_box, lhs, xs, pc, sel, q):
    def one(g, carry):
        base = g * 8
        weights = jnp.concatenate([xs[slot_box[base + i]] for i in range(8)], axis=0)
        rows = pl.ds(pl.multiple_of(base * CH, 64), 64)
        out = mm_nt(lhs[rows, :], weights)
        for i in range(8):
            tile = out[8 * i : 8 * i + 8, 128 * (i // 4) : 128 * (i // 4 + 1)]
            if i % 4:
                tile = pltpu.roll(tile, 128 - NB * (i % 4), 1)
            pc[pl.ds(base + i, CH, stride=SLOTS), :] = tile
        return carry

    lax.fori_loop(0, SLOTS // 8, one, 0, unroll=4)
    values = jnp.concatenate(
        [pc[SLOTS * c : SLOTS * (c + 1), 0:NB] for c in range(CH)], axis=1
    )
    hi, lo = split(values)
    q[...] = mm(sel[...], hi) + mm(sel[...], lo)


def couple(q, up, md, cf):
    total = q[ATOMS : 2 * ATOMS, :] + up[...]
    mixed = md[0] * total
    for d in range(1, CH):
        mixed = mixed + md[d] * pltpu.roll(total, NB * d, 1)
    cf[ATOMS : 2 * ATOMS, :] = mixed


def contribute(me, slot_atom, cf, k3, bw, cc):
    for c in range(CH):
        tile = cf[:, 128 * (c // 4) : 128 * (c // 4 + 1)]
        if c % 4:
            tile = pltpu.roll(tile, 128 - NB * (c % 4), 1)
        k3[:, c, :] = tile
    prev_start = lax.rem(me + NSLAB - 1, NSLAB) * ATOMS
    pair_of = lax.div(lax.rem(iota((NB, WIN), 1), 128), 16)

    def coefficients(k):
        atom = slot_atom[k]
        rel = atom - prev_start
        rel = jnp.where(rel < 0, rel + NATOM, rel)
        rel = jnp.where((atom < 0) | (rel >= 2 * ATOMS), 0, rel)
        return k3[rel]

    def one(g, carry):
        parts = []
        for i in range(8):
            parts.append(coefficients(g * 8 + i))
            parts.append(coefficients(HALF + g * 8 + i))
        turned = jnp.transpose(jnp.concatenate(parts, axis=0))[0:NB, :]
        hi = turned.astype(BF16).astype(F32)
        lo = turned - hi
        both = jnp.concatenate([hi, lo], axis=1)
        rows = jnp.concatenate(
            [jnp.where(pair_of == i, both, 0.0).astype(BF16) for i in range(8)], axis=0
        )
        weights = bw[g]
        out = mm(rows, jnp.concatenate([weights, weights], axis=0))
        cc[pl.ds(pl.multiple_of(g * 256, 256), 256), :] = out[:, 0:128] + out[:, 128:256]
        return carry

    lax.fori_loop(0, HALF // 8, one, 0, unroll=2)


def gather_boxes(n, cc, b4, y):
    low = iota((TILES, 128), 1) < 64
    hi, lo = split(cc[pl.ds(n, HALF, stride=NB), :])
    out = mm(b4[...], jnp.concatenate([hi, lo], axis=1))
    out = out[:, 0:128] + out[:, 128:256]
    stay = jnp.where(low, out[0:32], out[96:128])
    move = jnp.where(low, out[32:64], out[64:96])
    y[n] = stay + pltpu.roll(move, 64, 1)


def kernel(
    slot_atom, slot_box, meta, bands, projectors, coupling,
    out,
    xb, xs, pj, lf, lhs, bw, sel, b4, md, cw, pc, q, up, cf, k3, cc, y,
    in_send, in_recv, out_send, out_recv, up_send, up_recv, low_send, low_recv, load_sem, self_sem,
):
    me = lax.axis_index("slab")
    after = lax.rem(me + 1, NSLAB)
    before = lax.rem(me + NSLAB - 1, NSLAB)
    start = pl.multiple_of(jnp.minimum(lax.div(me * ATOMS, 128) * 128, NATOM - WIN), 128)
    load_slots = pltpu.make_async_copy(projectors, pj, load_sem.at[0])
    load_slots.start()
    load_mix = pltpu.make_async_copy(
        coupling.at[:, pl.ds(start, WIN)], cw.at[0:64, :], load_sem.at[1]
    )
    load_mix.start()

    barrier = pltpu.get_barrier_semaphore()

    def greet(i, carry):
        pl.semaphore_signal(
            barrier, inc=1, device_id={"slab": lax.rem(me + i, NSLAB)}, device_id_type=MESH
        )
        return carry

    lax.fori_loop(1, NSLAB, greet, 0)
    pl.semaphore_wait(barrier, NSLAB - 1)

    def rows_of(slab):
        return pl.ds(pl.multiple_of(slab * TILES, TILES), TILES)

    def self_in(blk):
        return pltpu.make_async_copy(
            bands.at[blk, rows_of(me), :], xb.at[blk, :, me, :], self_sem.at[blk]
        )

    def self_out(blk):
        return pltpu.make_async_copy(
            y.at[blk, me], out.at[blk, rows_of(me), :], self_sem.at[2 + blk]
        )

    def remote(src, dst, send_sem, recv_sem, peer):
        return pltpu.make_async_remote_copy(
            src, dst, send_sem, recv_sem, device_id={"slab": peer}, device_id_type=MESH
        )

    for blk in range(2):

        def send(i, carry):
            peer = lax.rem(me + i, NSLAB)
            remote(
                bands.at[blk, rows_of(peer), :],
                xb.at[blk, :, me, :],
                in_send.at[blk],
                in_recv.at[blk],
                peer,
            ).start()
            return carry

        lax.fori_loop(1, NSLAB, send, 0)
        self_in(blk).start()

    def whole(ref, sem):
        part = ref.at[0 : NSLAB - 1]
        return pltpu.make_async_copy(part, part, sem)

    def up_copy(blk):
        return remote(q.at[blk, 0:ATOMS], up.at[blk], up_send.at[blk], up_recv.at[blk], before)

    def low_copy(blk):
        return remote(
            cf.at[blk, ATOMS : 2 * ATOMS],
            cf.at[blk, 0:ATOMS],
            low_send.at[blk],
            low_recv.at[blk],
            after,
        )

    load_mix.wait()
    counts = meta[0:1, pl.ds(2 * SLOTS + start, WIN)].astype(F32)
    cw[64:72, :] = jnp.broadcast_to(counts, (8, WIN))
    prepare_tables(me, meta, cw, sel, b4, md, start)
    load_slots.wait()
    prepare_slots(pj, lf, lhs, bw)

    def project_block(blk):
        self_in(blk).wait()
        whole(xb.at[blk], in_recv.at[blk]).wait()
        split_bands(xb.at[blk], xs)
        project(slot_box, lhs, xs, pc, sel, q.at[blk])
        up_copy(blk).start()

    def couple_block(blk):
        up_copy(blk).wait_recv()
        couple(q.at[blk], up.at[blk], md, cf.at[blk])
        low_copy(blk).start()

    def apply_block(blk):
        low_copy(blk).wait_recv()
        contribute(me, slot_atom, cf.at[blk], k3, bw, cc)

        def ship(i, carry):
            peer = lax.rem(me + i, NSLAB)
            gather_boxes(peer, cc, b4, y.at[blk])
            remote(
                y.at[blk, peer],
                out.at[blk, rows_of(me), :],
                out_send.at[blk],
                out_recv.at[blk],
                peer,
            ).start()
            return carry

        lax.fori_loop(1, NSLAB, ship, 0)
        gather_boxes(me, cc, b4, y.at[blk])
        self_out(blk).start()

    project_block(0)
    couple_block(0)
    apply_block(0)
    project_block(1)
    couple_block(1)
    apply_block(1)

    for blk in range(2):
        whole(xb.at[blk], in_send.at[blk]).wait()
        up_copy(blk).wait_send()
        low_copy(blk).wait_send()
        self_out(blk).wait()
        whole(y.at[blk], out_send.at[blk]).wait()
        whole(y.at[blk], out_recv.at[blk]).wait()


def body(bands, projectors, slot_atom, slot_box, channels, coupling):
    nblock = bands.shape[0]
    ngrid = bands.shape[-1]
    meta = jnp.concatenate([slot_atom, slot_box, channels]).reshape(1, -1)
    any_space = pl.BlockSpec(memory_space=pl.ANY)
    smem = pl.BlockSpec(memory_space=pltpu.SMEM)
    vmem = pl.BlockSpec(memory_space=pltpu.VMEM)
    dma = pltpu.SemaphoreType.DMA
    result = pl.pallas_call(
        kernel,
        out_shape=jax.ShapeDtypeStruct((nblock, ngrid // 128, 128), F32),
        in_specs=[smem, smem, vmem, any_space, any_space, any_space],
        out_specs=any_space,
        scratch_shapes=[
            pltpu.VMEM((2, TILES, NB, 128), F32),
            pltpu.VMEM((BOXES, NB, 256), BF16),
            pltpu.VMEM((SLOTS, CH * PTS), F32),
            pltpu.VMEM((SLOTS * CH, 128), F32),
            pltpu.VMEM((SLOTS * CH, 256), BF16),
            pltpu.VMEM((HALF // 8, 128, 256), BF16),
            pltpu.VMEM((2 * ATOMS, SLOTS), BF16),
            pltpu.VMEM((4 * TILES, HALF), BF16),
            pltpu.VMEM((CH, ATOMS, CH * NB), F32),
            pltpu.VMEM((72, WIN), F32),
            pltpu.VMEM((CH * SLOTS, 128), F32),
            pltpu.VMEM((2, 2 * ATOMS, CH * NB), F32),
            pltpu.VMEM((2, ATOMS, CH * NB), F32),
            pltpu.VMEM((2, 2 * ATOMS, CH * NB), F32),
            pltpu.VMEM((2 * ATOMS, CH, 128), F32),
            pltpu.VMEM((HALF * NB, 128), F32),
            pltpu.VMEM((2, NSLAB, TILES, 128), F32),
            dma((2,)), dma((2,)), dma((2,)), dma((2,)),
            dma((2,)), dma((2,)), dma((2,)), dma((2,)),
            dma((2,)), dma((4,)),
        ],
        compiler_params=pltpu.CompilerParams(
            collective_id=0, has_side_effects=True, vmem_limit_bytes=60 * 1024 * 1024
        ),
        name="nonlocal",
    )(
        slot_atom,
        slot_box,
        meta,
        bands.reshape(nblock, ngrid // 128, 128),
        projectors,
        coupling.reshape(CH * CH, -1),
    )
    return result.reshape(bands.shape)


def solution(mesh):
    in_specs = (P(None, ("band", "slab"), None), P("slab", None), P("slab"), P("slab"), P(), P())
    out_specs = P(None, ("band", "slab"), None)
    return jax.shard_map(body, mesh=mesh, in_specs=in_specs, out_specs=out_specs, check_vma=False)
```

```python
import jax
import jax.numpy as jnp
from jax import lax
from jax.experimental import pallas as pl
from jax.experimental.pallas import tpu as pltpu
from jax.sharding import PartitionSpec as P

MESH = pl.DeviceIdType.MESH
F32 = jnp.float32
BF16 = jnp.bfloat16
NSLAB = 32
PTS = 64
BOXES = 64
TILES = BOXES // 2
SLOTS = 512
HALF = SLOTS // 2
CH = 8
ATOMS = 96
NATOM = NSLAB * ATOMS
NB = 32
STEP = 40
WIN = 256


def split(x):
    hi = x.astype(BF16)
    lo = (x - hi.astype(F32)).astype(BF16)
    return hi, lo


def mm(a, b):
    return jnp.dot(a, b, preferred_element_type=F32)


def mm_nt(a, b, precision=None):
    return lax.dot_general(
        a, b, (((1,), (1,)), ((), ())), preferred_element_type=F32, precision=precision
    )


def iota(shape, axis):
    return lax.broadcasted_iota(jnp.int32, shape, axis)


def prepare_rows(me, slot_atom, rows_at):
    prev_start = lax.rem(me + NSLAB - 1, NSLAB) * ATOMS

    def one(k, carry):
        atom = slot_atom[k]
        rel = atom - prev_start
        rel = jnp.where(rel < 0, rel + NATOM, rel)
        rows_at[k] = jnp.where((atom < 0) | (rel >= 2 * ATOMS), 0, rel)
        return carry

    lax.fori_loop(0, SLOTS, one, 0, unroll=8)


def prepare_slots(pj, lf, lhs, bw):
    for q in range(4):
        v = pj[:, 128 * q : 128 * (q + 1)]
        lf[pl.ds(2 * q, SLOTS, stride=CH), :] = v
        lf[pl.ds(2 * q + 1, SLOTS, stride=CH), :] = pltpu.roll(v, 64, 1)
    low = iota((128, 128), 1) < 64

    def one(i, carry):
        rows = pl.ds(pl.multiple_of(i * 128, 128), 128)
        x = lf[rows, :]
        both = jnp.where(low, x, pltpu.roll(x, 64, 1))
        hi = both.astype(BF16).astype(F32)
        lo = both - hi
        lhs[rows, 0:128] = hi.astype(BF16)
        lhs[rows, 128:256] = jnp.where(low, lo, 0.0).astype(BF16)
        lf[rows, :] = both
        return carry

    lax.fori_loop(0, SLOTS * CH // 128, one, 0, unroll=2)
    keep = (iota((16, 128), 0) < 8) == (iota((16, 128), 1) < 64)

    def two(g, carry):
        for i in range(8):
            first = pl.multiple_of((g * 8 + i) * CH, CH)
            second = pl.multiple_of((HALF + g * 8 + i) * CH, CH)
            x = jnp.concatenate([lf[pl.ds(first, CH), :], lf[pl.ds(second, CH), :]], axis=0)
            x = jnp.where(keep, x, 0.0)
            hi = x.astype(BF16)
            lo = (x - hi.astype(F32)).astype(BF16)
            bw[g, 16 * i : 16 * (i + 1), 0:128] = hi
            bw[g, 16 * i : 16 * (i + 1), 128:256] = lo
        return carry

    lax.fori_loop(0, HALF // 8, two, 0)


def prepare_tables(me, meta, cw, sel, b4, md, start):
    slot_atom = meta[0:1, 0:SLOTS]
    slot_box = meta[0:1, SLOTS : 2 * SLOTS]
    live = slot_atom >= 0
    prev_start = lax.rem(me + NSLAB - 1, NSLAB) * ATOMS
    rel = slot_atom - prev_start
    rel = jnp.where(rel < 0, rel + NATOM, rel)
    rel = jnp.where(live, rel, -1)
    sel[...] = jnp.where(iota((2 * ATOMS, SLOTS), 0) == rel, 1.0, 0.0).astype(BF16)
    box = jnp.where(live, slot_box, -1)
    row = iota((TILES, HALF), 0)
    for i2 in range(2):
        part = box[:, HALF * i2 : HALF * (i2 + 1)]
        for p in range(2):
            at = (2 * i2 + p) * TILES
            b4[at : at + TILES, :] = jnp.where(2 * row + p == part, 1.0, 0.0).astype(BF16)
    offset = me * ATOMS - start
    own = jnp.where(iota((ATOMS, WIN), 1) == iota((ATOMS, WIN), 0) + offset, 1.0, 0.0)
    mixing = mm_nt(own, cw[0:72, :], lax.Precision.HIGHEST)
    count = mixing[:, 64:65]
    pair_channel = iota((ATOMS, 64), 1)
    keep = (lax.div(pair_channel, CH).astype(F32) < count) & (
        lax.rem(pair_channel, CH).astype(F32) < count
    )
    mixing = jnp.where(keep, mixing[:, 0:64], 0.0)
    pair = iota((64, CH * NB), 0)
    to = lax.div(iota((64, CH * NB), 1), NB)
    for d in range(CH):
        source = lax.rem(to + CH - d, CH)
        spread = jnp.where(pair == to * CH + source, 1.0, 0.0)
        md[d] = jnp.dot(
            mixing, spread, preferred_element_type=F32, precision=lax.Precision.HIGHEST
        )


def split_bands(xb, xs):
    low = iota((NB, 128), 1) < 64

    def one(r, carry):
        x = xb[r]
        turned = pltpu.roll(x, 64, 1)
        for p in range(2):
            both = jnp.where(low, x, turned) if p == 0 else jnp.where(low, turned, x)
            hi = both.astype(BF16).astype(F32)
            lo = both - hi
            xs[2 * r + p, :, 0:128] = jnp.where(low, hi, lo).astype(BF16)
            xs[2 * r + p, :, 128:256] = hi.astype(BF16)
        return carry

    lax.fori_loop(0, TILES, one, 0, unroll=8)


def project(slot_box, lhs, xs, pc, sel, q):
    def one(g, carry):
        base = g * 8
        weights = jnp.concatenate([xs[slot_box[base + i]] for i in range(8)], axis=0)
        rows = pl.ds(pl.multiple_of(base * CH, 64), 64)
        out = mm_nt(lhs[rows, :], weights)
        for i in range(8):
            tile = out[8 * i : 8 * i + 8, 128 * (i // 4) : 128 * (i // 4 + 1)]
            if i % 4:
                tile = pltpu.roll(tile, 128 - NB * (i % 4), 1)
            pc[pl.ds(base + i, CH, stride=SLOTS), :] = tile
        return carry

    lax.fori_loop(0, SLOTS // 8, one, 0, unroll=16)
    values = jnp.concatenate(
        [pc[SLOTS * c : SLOTS * (c + 1), 0:NB] for c in range(CH)], axis=1
    )
    hi, lo = split(values)
    q[...] = mm(sel[...], hi) + mm(sel[...], lo)


def couple(q, up, md, cf):
    total = q[ATOMS : 2 * ATOMS, :] + up[...]
    mixed = md[0] * total
    for d in range(1, CH):
        mixed = mixed + md[d] * pltpu.roll(total, NB * d, 1)
    cf[ATOMS : 2 * ATOMS, :] = mixed


def contribute(rows_at, cf, k3, bw, cc):
    for c in range(CH):
        tile = cf[:, 128 * (c // 4) : 128 * (c // 4 + 1)]
        if c % 4:
            tile = pltpu.roll(tile, 128 - NB * (c % 4), 1)
        k3[:, c, :] = tile
    pair_of = lax.div(lax.rem(iota((NB, WIN), 1), 128), 16)

    def one(g, carry):
        parts = []
        for i in range(8):
            parts.append(k3[rows_at[g * 8 + i]])
            parts.append(k3[rows_at[HALF + g * 8 + i]])
        turned = jnp.transpose(jnp.concatenate(parts, axis=0))[0:NB, :]
        hi = turned.astype(BF16).astype(F32)
        lo = turned - hi
        both = jnp.concatenate([hi, lo], axis=1)
        rows = jnp.concatenate(
            [jnp.where(pair_of == i, both, 0.0).astype(BF16) for i in range(8)], axis=0
        )
        weights = bw[g]
        out = mm(rows, jnp.concatenate([weights, weights], axis=0))
        out = out[:, 0:128] + out[:, 128:256]
        for i in range(8):
            first = pl.multiple_of((g * 8 + i) * STEP, 8)
            cc[pl.ds(first, NB), :] = out[NB * i : NB * (i + 1), :]
        return carry

    lax.fori_loop(0, HALF // 8, one, 0, unroll=8)


def gather_boxes(n, cc, b4, y):
    low = iota((TILES, 128), 1) < 64
    hi, lo = split(cc[pl.ds(n, HALF, stride=STEP), :])
    out = mm(b4[...], jnp.concatenate([hi, lo], axis=1))
    out = out[:, 0:128] + out[:, 128:256]
    stay = jnp.where(low, out[0:32], out[96:128])
    move = jnp.where(low, out[32:64], out[64:96])
    y[n] = stay + pltpu.roll(move, 64, 1)


def kernel(
    slot_atom, slot_box, meta, bands, projectors, coupling,
    out,
    xb, xs, pj, lf, lhs, bw, sel, b4, md, cw, pc, q, up, cf, k3, cc, y, rows_at,
    in_send, in_recv, out_send, out_recv, up_send, up_recv, low_send, low_recv, load_sem, self_sem,
):
    me = lax.axis_index("slab")
    after = lax.rem(me + 1, NSLAB)
    before = lax.rem(me + NSLAB - 1, NSLAB)
    start = pl.multiple_of(jnp.minimum(lax.div(me * ATOMS, 128) * 128, NATOM - WIN), 128)
    load_slots = pltpu.make_async_copy(projectors, pj, load_sem.at[0])
    load_slots.start()
    load_mix = pltpu.make_async_copy(
        coupling.at[:, pl.ds(start, WIN)], cw.at[0:64, :], load_sem.at[1]
    )
    load_mix.start()

    barrier = pltpu.get_barrier_semaphore()

    def greet(i, carry):
        pl.semaphore_signal(
            barrier, inc=1, device_id={"slab": lax.rem(me + i, NSLAB)}, device_id_type=MESH
        )
        return carry

    lax.fori_loop(1, NSLAB, greet, 0)
    pl.semaphore_wait(barrier, NSLAB - 1)

    def rows_of(slab):
        return pl.ds(pl.multiple_of(slab * TILES, TILES), TILES)

    def self_in(blk):
        return pltpu.make_async_copy(
            bands.at[blk, rows_of(me), :], xb.at[blk, :, me, :], self_sem.at[blk]
        )

    def self_out(blk):
        return pltpu.make_async_copy(
            y.at[blk, me], out.at[blk, rows_of(me), :], self_sem.at[2 + blk]
        )

    def remote(src, dst, send_sem, recv_sem, peer):
        return pltpu.make_async_remote_copy(
            src, dst, send_sem, recv_sem, device_id={"slab": peer}, device_id_type=MESH
        )

    for blk in range(2):

        def send(i, carry):
            peer = lax.rem(me + i, NSLAB)
            remote(
                bands.at[blk, rows_of(peer), :],
                xb.at[blk, :, me, :],
                in_send.at[blk],
                in_recv.at[blk],
                peer,
            ).start()
            return carry

        lax.fori_loop(1, NSLAB, send, 0)
        self_in(blk).start()

    def whole(ref, sem):
        part = ref.at[0 : NSLAB - 1]
        return pltpu.make_async_copy(part, part, sem)

    def up_copy(blk):
        return remote(q.at[blk, 0:ATOMS], up.at[blk], up_send.at[blk], up_recv.at[blk], before)

    def low_copy(blk):
        return remote(
            cf.at[blk, ATOMS : 2 * ATOMS],
            cf.at[blk, 0:ATOMS],
            low_send.at[blk],
            low_recv.at[blk],
            after,
        )

    load_mix.wait()
    counts = meta[0:1, pl.ds(2 * SLOTS + start, WIN)].astype(F32)
    cw[64:72, :] = jnp.broadcast_to(counts, (8, WIN))
    prepare_rows(me, slot_atom, rows_at)
    prepare_tables(me, meta, cw, sel, b4, md, start)
    load_slots.wait()
    prepare_slots(pj, lf, lhs, bw)

    def project_block(blk):
        self_in(blk).wait()
        whole(xb.at[blk], in_recv.at[blk]).wait()
        split_bands(xb.at[blk], xs)
        project(slot_box, lhs, xs, pc, sel, q.at[blk])
        up_copy(blk).start()

    def couple_block(blk):
        up_copy(blk).wait_recv()
        couple(q.at[blk], up.at[blk], md, cf.at[blk])
        low_copy(blk).start()

    def apply_block(blk):
        low_copy(blk).wait_recv()
        contribute(rows_at, cf.at[blk], k3, bw, cc)

        def ship(i):
            peer = lax.rem(me + i, NSLAB)
            remote(
                y.at[blk, peer],
                out.at[blk, rows_of(me), :],
                out_send.at[blk],
                out_recv.at[blk],
                peer,
            ).start()

        def eight(g, carry):
            for i in range(1, 9):
                gather_boxes(lax.rem(me + g * 8 + i, NSLAB), cc, b4, y.at[blk])
            for i in range(1, 9):
                ship(g * 8 + i)
            return carry

        lax.fori_loop(0, 3, eight, 0)
        for i in range(25, 33):
            gather_boxes(lax.rem(me + i, NSLAB), cc, b4, y.at[blk])
        for i in range(25, 32):
            ship(i)
        self_out(blk).start()

    project_block(0)
    couple_block(0)
    apply_block(0)
    project_block(1)
    couple_block(1)
    apply_block(1)

    for blk in range(2):
        whole(xb.at[blk], in_send.at[blk]).wait()
        up_copy(blk).wait_send()
        low_copy(blk).wait_send()
        self_out(blk).wait()
        whole(y.at[blk], out_send.at[blk]).wait()
        whole(y.at[blk], out_recv.at[blk]).wait()


def body(bands, projectors, slot_atom, slot_box, channels, coupling):
    nblock = bands.shape[0]
    ngrid = bands.shape[-1]
    meta = jnp.concatenate([slot_atom, slot_box, channels]).reshape(1, -1)
    any_space = pl.BlockSpec(memory_space=pl.ANY)
    smem = pl.BlockSpec(memory_space=pltpu.SMEM)
    vmem = pl.BlockSpec(memory_space=pltpu.VMEM)
    dma = pltpu.SemaphoreType.DMA
    result = pl.pallas_call(
        kernel,
        out_shape=jax.ShapeDtypeStruct((nblock, ngrid // 128, 128), F32),
        in_specs=[smem, smem, vmem, any_space, any_space, any_space],
        out_specs=any_space,
        scratch_shapes=[
            pltpu.VMEM((2, TILES, NB, 128), F32),
            pltpu.VMEM((BOXES, NB, 256), BF16),
            pltpu.VMEM((SLOTS, CH * PTS), F32),
            pltpu.VMEM((SLOTS * CH, 128), F32),
            pltpu.VMEM((SLOTS * CH, 256), BF16),
            pltpu.VMEM((HALF // 8, 128, 256), BF16),
            pltpu.VMEM((2 * ATOMS, SLOTS), BF16),
            pltpu.VMEM((4 * TILES, HALF), BF16),
            pltpu.VMEM((CH, ATOMS, CH * NB), F32),
            pltpu.VMEM((72, WIN), F32),
            pltpu.VMEM((CH * SLOTS, 128), F32),
            pltpu.VMEM((2, 2 * ATOMS, CH * NB), F32),
            pltpu.VMEM((2, ATOMS, CH * NB), F32),
            pltpu.VMEM((2, 2 * ATOMS, CH * NB), F32),
            pltpu.VMEM((2 * ATOMS, CH, 128), F32),
            pltpu.VMEM((HALF * STEP, 128), F32),
            pltpu.VMEM((2, NSLAB, TILES, 128), F32),
            pltpu.SMEM((SLOTS,), jnp.int32),
            dma((2,)), dma((2,)), dma((2,)), dma((2,)),
            dma((2,)), dma((2,)), dma((2,)), dma((2,)),
            dma((2,)), dma((4,)),
        ],
        compiler_params=pltpu.CompilerParams(
            collective_id=0, has_side_effects=True, vmem_limit_bytes=60 * 1024 * 1024
        ),
        name="nonlocal",
    )(
        slot_atom,
        slot_box,
        meta,
        bands.reshape(nblock, ngrid // 128, 128),
        projectors,
        coupling.reshape(CH * CH, -1),
    )
    return result.reshape(bands.shape)


def solution(mesh):
    in_specs = (P(None, ("band", "slab"), None), P("slab", None), P("slab"), P("slab"), P(), P())
    out_specs = P(None, ("band", "slab"), None)
    return jax.shard_map(body, mesh=mesh, in_specs=in_specs, out_specs=out_specs, check_vma=False)
```

```python
import jax
import jax.numpy as jnp
from jax import lax
from jax.experimental import pallas as pl
from jax.experimental.pallas import tpu as pltpu
from jax.sharding import PartitionSpec as P

MESH = pl.DeviceIdType.MESH
F32 = jnp.float32
BF16 = jnp.bfloat16
NSLAB = 32
PTS = 64
BOXES = 64
TILES = BOXES // 2
SLOTS = 512
HALF = SLOTS // 2
CH = 8
ATOMS = 96
NATOM = NSLAB * ATOMS
NB = 32
STEP = 40
PARTS = 3
EARLY = 22
PART = ATOMS // PARTS
WIN = 256


def split(x):
    hi = x.astype(BF16)
    lo = (x - hi.astype(F32)).astype(BF16)
    return hi, lo


def mm(a, b):
    return jnp.dot(a, b, preferred_element_type=F32)


def mm_nt(a, b, precision=None):
    return lax.dot_general(
        a, b, (((1,), (1,)), ((), ())), preferred_element_type=F32, precision=precision
    )


def iota(shape, axis):
    return lax.broadcasted_iota(jnp.int32, shape, axis)


def distance(i):
    block = lax.div(i - 1, 2)
    side = lax.rem(i - 1, 2)
    far = lax.rem(block, 2)
    step = lax.div(block, 2)
    hops = (1 + step) * (1 - far) + (15 - step) * far
    return hops * (1 - side) + (NSLAB - hops) * side


def prepare_rows(me, slot_atom, rows_at):
    prev_start = lax.rem(me + NSLAB - 1, NSLAB) * ATOMS

    def one(k, carry):
        atom = slot_atom[k]
        rel = atom - prev_start
        rel = jnp.where(rel < 0, rel + NATOM, rel)
        rows_at[k] = jnp.where((atom < 0) | (rel >= 2 * ATOMS), 0, rel)
        return carry

    lax.fori_loop(0, SLOTS, one, 0, unroll=8)


def prepare_slots(pj, lf, lhs, bw):
    for q in range(4):
        v = pj[:, 128 * q : 128 * (q + 1)]
        lf[pl.ds(2 * q, SLOTS, stride=CH), :] = v
        lf[pl.ds(2 * q + 1, SLOTS, stride=CH), :] = pltpu.roll(v, 64, 1)
    low = iota((128, 128), 1) < 64

    def one(i, carry):
        rows = pl.ds(pl.multiple_of(i * 128, 128), 128)
        x = lf[rows, :]
        both = jnp.where(low, x, pltpu.roll(x, 64, 1))
        hi = both.astype(BF16).astype(F32)
        lo = both - hi
        lhs[rows, 0:128] = hi.astype(BF16)
        lhs[rows, 128:256] = jnp.where(low, lo, 0.0).astype(BF16)
        lf[rows, :] = both
        return carry

    lax.fori_loop(0, SLOTS * CH // 128, one, 0, unroll=2)
    keep = (iota((16, 128), 0) < 8) == (iota((16, 128), 1) < 64)

    def two(g, carry):
        for i in range(8):
            first = pl.multiple_of((g * 8 + i) * CH, CH)
            second = pl.multiple_of((HALF + g * 8 + i) * CH, CH)
            x = jnp.concatenate([lf[pl.ds(first, CH), :], lf[pl.ds(second, CH), :]], axis=0)
            x = jnp.where(keep, x, 0.0)
            hi = x.astype(BF16)
            lo = (x - hi.astype(F32)).astype(BF16)
            bw[g, 16 * i : 16 * (i + 1), 0:128] = hi
            bw[g, 16 * i : 16 * (i + 1), 128:256] = lo
        return carry

    lax.fori_loop(0, HALF // 8, two, 0)


def prepare_tables(me, atom_row, box_row, cw, sel, b4, md, start):
    slot_atom = atom_row[...]
    slot_box = box_row[...]
    live = slot_atom >= 0
    prev_start = lax.rem(me + NSLAB - 1, NSLAB) * ATOMS
    rel = slot_atom - prev_start
    rel = jnp.where(rel < 0, rel + NATOM, rel)
    rel = jnp.where(live, rel, -1)
    sel[...] = jnp.where(iota((2 * ATOMS, SLOTS), 0) == rel, 1.0, 0.0).astype(BF16)
    box = jnp.where(live, slot_box, -1)
    row = iota((TILES, HALF), 0)
    for i2 in range(2):
        part = box[:, HALF * i2 : HALF * (i2 + 1)]
        for p in range(2):
            at = (2 * i2 + p) * TILES
            b4[at : at + TILES, :] = jnp.where(2 * row + p == part, 1.0, 0.0).astype(BF16)
    offset = me * ATOMS - start
    own = jnp.where(iota((ATOMS, WIN), 1) == iota((ATOMS, WIN), 0) + offset, 1.0, 0.0)
    mixing = mm_nt(own, cw[0:72, :], lax.Precision.HIGHEST)
    count = mixing[:, 64:65]
    pair_channel = iota((ATOMS, 64), 1)
    keep = (lax.div(pair_channel, CH).astype(F32) < count) & (
        lax.rem(pair_channel, CH).astype(F32) < count
    )
    mixing = jnp.where(keep, mixing[:, 0:64], 0.0)
    pair = iota((64, CH * NB), 0)
    to = lax.div(iota((64, CH * NB), 1), NB)
    for d in range(CH):
        source = lax.rem(to + CH - d, CH)
        spread = jnp.where(pair == to * CH + source, 1.0, 0.0)
        md[d] = jnp.dot(
            mixing, spread, preferred_element_type=F32, precision=lax.Precision.HIGHEST
        )


def split_bands(xb, xs):
    low = iota((NB, 128), 1) < 64

    def one(r, carry):
        x = xb[r]
        turned = pltpu.roll(x, 64, 1)
        for p in range(2):
            both = jnp.where(low, x, turned) if p == 0 else jnp.where(low, turned, x)
            hi = both.astype(BF16).astype(F32)
            lo = both - hi
            xs[2 * r + p, :, 0:128] = jnp.where(low, hi, lo).astype(BF16)
            xs[2 * r + p, :, 128:256] = hi.astype(BF16)
        return carry

    lax.fori_loop(0, TILES, one, 0, unroll=8)


def project(slot_box, lhs, xs, pc, sel, q, between):
    def group(g):
        base = g * 8
        weights = jnp.concatenate([xs[slot_box[base + i]] for i in range(8)], axis=0)
        rows = pl.ds(pl.multiple_of(base * CH, 64), 64)
        out = mm_nt(lhs[rows, :], weights)
        for i in range(8):
            tile = out[8 * i : 8 * i + 8, 128 * (i // 4) : 128 * (i // 4 + 1)]
            if i % 4:
                tile = pltpu.roll(tile, 128 - NB * (i % 4), 1)
            pc[pl.ds(base + i, CH, stride=SLOTS), :] = tile

    def part(j, carry):
        for i in range(16):
            group(j * 16 + i)
        return carry

    lax.fori_loop(0, SLOTS // 128, part, 0)
    values = jnp.concatenate(
        [pc[SLOTS * c : SLOTS * (c + 1), 0:NB] for c in range(CH)], axis=1
    )
    hi, lo = split(values)
    for j in range(PARTS):
        rows = slice(PART * j, PART * (j + 1))
        q[rows, :] = mm(sel[rows, :], hi) + mm(sel[rows, :], lo)
        between(j)
    rows = slice(ATOMS, 2 * ATOMS)
    q[rows, :] = mm(sel[rows, :], hi) + mm(sel[rows, :], lo)


def couple(j, q, up, md, cf):
    rows = slice(PART * j, PART * (j + 1))
    own = slice(ATOMS + PART * j, ATOMS + PART * (j + 1))
    total = q[own, :] + up[rows, :]
    mixed = md[0, rows] * total
    for d in range(1, CH):
        mixed = mixed + md[d, rows] * pltpu.roll(total, NB * d, 1)
    cf[own, :] = mixed


def spread_rows(first, cf, k3):
    rows = slice(first, first + ATOMS)
    for c in range(CH):
        tile = cf[rows, 128 * (c // 4) : 128 * (c // 4 + 1)]
        if c % 4:
            tile = pltpu.roll(tile, 128 - NB * (c % 4), 1)
        k3[rows, c, :] = tile


def contribute(rows_at, k3, bw, cc):
    pair_of = lax.div(lax.rem(iota((NB, WIN), 1), 128), 16)

    def one(g, carry):
        parts = []
        for i in range(8):
            parts.append(k3[rows_at[g * 8 + i]])
            parts.append(k3[rows_at[HALF + g * 8 + i]])
        turned = jnp.transpose(jnp.concatenate(parts, axis=0))[0:NB, :]
        hi = turned.astype(BF16).astype(F32)
        lo = turned - hi
        both = jnp.concatenate([hi, lo], axis=1)
        rows = jnp.concatenate(
            [jnp.where(pair_of == i, both, 0.0).astype(BF16) for i in range(8)], axis=0
        )
        weights = bw[g]
        out = mm(rows, jnp.concatenate([weights, weights], axis=0))
        out = out[:, 0:128] + out[:, 128:256]
        for i in range(8):
            first = pl.multiple_of((g * 8 + i) * STEP, 8)
            cc[pl.ds(first, NB), :] = out[NB * i : NB * (i + 1), :]
        return carry

    lax.fori_loop(0, HALF // 8, one, 0, unroll=8)


def gather_boxes(n, cc, b4, y):
    low = iota((TILES, 128), 1) < 64
    hi, lo = split(cc[pl.ds(n, HALF, stride=STEP), :])
    out = mm(b4[...], jnp.concatenate([hi, lo], axis=1))
    out = out[:, 0:128] + out[:, 128:256]
    stay = jnp.where(low, out[0:32], out[96:128])
    move = jnp.where(low, out[32:64], out[64:96])
    y[n] = stay + pltpu.roll(move, 64, 1)


def kernel(
    slot_atom, slot_box, channels, bands, projectors, coupling,
    out,
    atom_row, box_row, count_row, atom_at, box_at, rows_at,
    xb, xs, pj, lf, lhs, bw, sel, b4, md, cw, pc, q, up, cf, k3, cc, y,
    in_send, in_recv, out_send, out_recv, up_send, up_recv, low_send, low_recv, load_sem, self_sem,
):
    me = lax.axis_index("slab")
    after = lax.rem(me + 1, NSLAB)
    before = lax.rem(me + NSLAB - 1, NSLAB)
    start = pl.multiple_of(jnp.minimum(lax.div(me * ATOMS, 128) * 128, NATOM - WIN), 128)

    barrier = pltpu.get_barrier_semaphore()

    def greet(i, carry):
        pl.semaphore_signal(
            barrier, inc=1, device_id={"slab": lax.rem(me + i, NSLAB)}, device_id_type=MESH
        )
        return carry

    lax.fori_loop(1, NSLAB, greet, 0)

    loads = [
        pltpu.make_async_copy(src, dst, load_sem.at[i])
        for i, (src, dst) in enumerate(
            [
                (slot_atom, atom_row),
                (slot_box, box_row),
                (channels.at[:, pl.ds(start, WIN)], count_row),
                (slot_atom.at[0], atom_at),
                (slot_box.at[0], box_at),
                (coupling.at[:, pl.ds(start, WIN)], cw.at[0:64, :]),
                (projectors, pj),
            ]
        )
    ]
    for load in loads:
        load.start()
    pl.semaphore_wait(barrier, NSLAB - 1)

    def rows_of(slab):
        return pl.ds(pl.multiple_of(slab * TILES, TILES), TILES)

    def self_in(blk):
        return pltpu.make_async_copy(
            bands.at[blk, rows_of(me), :], xb.at[blk, :, me, :], self_sem.at[blk]
        )

    def self_out(blk):
        return pltpu.make_async_copy(
            y.at[blk, me], out.at[blk, rows_of(me), :], self_sem.at[2 + blk]
        )

    def remote(src, dst, send_sem, recv_sem, peer):
        return pltpu.make_async_remote_copy(
            src, dst, send_sem, recv_sem, device_id={"slab": peer}, device_id_type=MESH
        )

    def send_in(blk, offset, batch):
        peer = lax.rem(me + offset, NSLAB)
        remote(
            bands.at[blk, rows_of(peer), :],
            xb.at[blk, :, me, :],
            in_send.at[batch],
            in_recv.at[blk],
            peer,
        ).start()

    def send_out(blk, offset):
        peer = lax.rem(me + offset, NSLAB)
        remote(
            y.at[blk, peer],
            out.at[blk, rows_of(me), :],
            out_send.at[blk],
            out_recv.at[blk],
            peer,
        ).start()

    def some(send, first, count):
        def one(i, carry):
            send(distance(first + i))
            return carry

        lax.fori_loop(0, count, one, 0)

    def bytes_of(ref, count, sem):
        part = ref.at[0:count]
        return pltpu.make_async_copy(part, part, sem)

    send_in(0, 16, 0)
    some(lambda offset: send_in(0, offset, 0), 1, EARLY - 1)
    some(lambda offset: send_in(0, offset, 1), EARLY, NSLAB - 1 - EARLY)
    self_in(0).start()
    self_in(1).start()

    def up_copy(blk, j):
        rows = slice(PART * j, PART * (j + 1))
        return remote(
            q.at[blk, rows], up.at[blk, rows], up_send.at[blk, j], up_recv.at[blk, j], before
        )

    def low_copy(blk, j):
        return remote(
            cf.at[blk, ATOMS + PART * j : ATOMS + PART * (j + 1)],
            cf.at[blk, PART * j : PART * (j + 1)],
            low_send.at[blk, j],
            low_recv.at[blk, j],
            after,
        )

    for load in loads:
        load.wait()
    prepare_slots(pj, lf, lhs, bw)
    cw[64:72, :] = jnp.broadcast_to(count_row[...].astype(F32), (8, WIN))
    prepare_tables(me, atom_row, box_row, cw, sel, b4, md, start)
    prepare_rows(me, atom_at, rows_at)
    bytes_of(xb.at[0], EARLY, in_send.at[0]).wait()
    send_in(1, 16, 2)
    some(lambda offset: send_in(1, offset, 2), 1, NSLAB - 2)

    def gather(blk, offset):
        gather_boxes(lax.rem(me + offset, NSLAB), cc, b4, y.at[blk])

    def process(blk):
        self_in(blk).wait()
        bytes_of(xb.at[blk], NSLAB - 1, in_recv.at[blk]).wait()
        split_bands(xb.at[blk], xs)
        project(box_at, lhs, xs, pc, sel, q.at[blk], lambda j: up_copy(blk, j).start())
        for j in range(PARTS):
            up_copy(blk, j).wait_recv()
            couple(j, q.at[blk], up.at[blk], md, cf.at[blk])
            low_copy(blk, j).start()
        spread_rows(ATOMS, cf.at[blk], k3)
        for j in range(PARTS):
            low_copy(blk, j).wait_recv()
        spread_rows(0, cf.at[blk], k3)
        contribute(rows_at, k3, bw, cc)

        def eight(g, carry):
            for i in range(8):
                gather(blk, distance(1 + 8 * g + i))
            some(lambda offset: send_out(blk, offset), 1 + 8 * g, 8)
            return carry

        lax.fori_loop(0, 3, eight, 0)
        for i in range(25, 31):
            gather(blk, distance(i))
        gather(blk, 16)
        gather(blk, 0)
        some(lambda offset: send_out(blk, offset), 25, 6)
        send_out(blk, 16)
        self_out(blk).start()

    process(0)
    process(1)

    bytes_of(xb.at[0], NSLAB - 1 - EARLY, in_send.at[1]).wait()
    bytes_of(xb.at[1], NSLAB - 1, in_send.at[2]).wait()
    for blk in range(2):
        for j in range(PARTS):
            up_copy(blk, j).wait_send()
            low_copy(blk, j).wait_send()
        self_out(blk).wait()
        bytes_of(y.at[blk], NSLAB - 1, out_send.at[blk]).wait()
        bytes_of(y.at[blk], NSLAB - 1, out_recv.at[blk]).wait()


def body(bands, projectors, slot_atom, slot_box, channels, coupling):
    nblock = bands.shape[0]
    ngrid = bands.shape[-1]
    any_space = pl.BlockSpec(memory_space=pl.ANY)
    dma = pltpu.SemaphoreType.DMA
    result = pl.pallas_call(
        kernel,
        out_shape=jax.ShapeDtypeStruct((nblock, ngrid // 128, 128), F32),
        in_specs=[any_space] * 6,
        out_specs=any_space,
        scratch_shapes=[
            pltpu.VMEM((1, SLOTS), jnp.int32),
            pltpu.VMEM((1, SLOTS), jnp.int32),
            pltpu.VMEM((1, WIN), jnp.int32),
            pltpu.SMEM((SLOTS,), jnp.int32),
            pltpu.SMEM((SLOTS,), jnp.int32),
            pltpu.SMEM((SLOTS,), jnp.int32),
            pltpu.VMEM((2, TILES, NB, 128), F32),
            pltpu.VMEM((BOXES, NB, 256), BF16),
            pltpu.VMEM((SLOTS, CH * PTS), F32),
            pltpu.VMEM((SLOTS * CH, 128), F32),
            pltpu.VMEM((SLOTS * CH, 256), BF16),
            pltpu.VMEM((HALF // 8, 128, 256), BF16),
            pltpu.VMEM((2 * ATOMS, SLOTS), BF16),
            pltpu.VMEM((4 * TILES, HALF), BF16),
            pltpu.VMEM((CH, ATOMS, CH * NB), F32),
            pltpu.VMEM((72, WIN), F32),
            pltpu.VMEM((CH * SLOTS, 128), F32),
            pltpu.VMEM((2, 2 * ATOMS, CH * NB), F32),
            pltpu.VMEM((2, ATOMS, CH * NB), F32),
            pltpu.VMEM((2, 2 * ATOMS, CH * NB), F32),
            pltpu.VMEM((2 * ATOMS, CH, 128), F32),
            pltpu.VMEM((HALF * STEP, 128), F32),
            pltpu.VMEM((2, NSLAB, TILES, 128), F32),
            dma((3,)), dma((2,)), dma((2,)), dma((2,)),
            dma((2, PARTS)), dma((2, PARTS)), dma((2, PARTS)), dma((2, PARTS)),
            dma((7,)), dma((4,)),
        ],
        compiler_params=pltpu.CompilerParams(
            collective_id=0, has_side_effects=True, vmem_limit_bytes=60 * 1024 * 1024
        ),
        name="nonlocal",
    )(
        slot_atom.reshape(1, -1),
        slot_box.reshape(1, -1),
        channels.reshape(1, -1),
        bands.reshape(nblock, ngrid // 128, 128),
        projectors,
        coupling.reshape(CH * CH, -1),
    )
    return result.reshape(bands.shape)


def solution(mesh):
    in_specs = (P(None, ("band", "slab"), None), P("slab", None), P("slab"), P("slab"), P(), P())
    out_specs = P(None, ("band", "slab"), None)
    return jax.shard_map(body, mesh=mesh, in_specs=in_specs, out_specs=out_specs, check_vma=False)
```

```python
import jax
import jax.numpy as jnp
from jax import lax
from jax.experimental import pallas as pl
from jax.experimental.pallas import tpu as pltpu
from jax.sharding import PartitionSpec as P

MESH = pl.DeviceIdType.MESH
F32 = jnp.float32
BF16 = jnp.bfloat16
NSLAB = 32
PTS = 64
BOXES = 64
TILES = BOXES // 2
SLOTS = 512
HALF = SLOTS // 2
CH = 8
ATOMS = 96
NATOM = NSLAB * ATOMS
NB = 32
STEP = 40
PARTS = 3
EARLY = 12
PART = ATOMS // PARTS
WIN = 256


def split(x):
    hi = x.astype(BF16)
    lo = (x - hi.astype(F32)).astype(BF16)
    return hi, lo


def mm(a, b):
    return jnp.dot(a, b, preferred_element_type=F32)


def mm_nt(a, b, precision=None):
    return lax.dot_general(
        a, b, (((1,), (1,)), ((), ())), preferred_element_type=F32, precision=precision
    )


def iota(shape, axis):
    return lax.broadcasted_iota(jnp.int32, shape, axis)


def distance(i):
    block = lax.div(i - 1, 2)
    side = lax.rem(i - 1, 2)
    far = lax.rem(block, 2)
    step = lax.div(block, 2)
    hops = (1 + step) * (1 - far) + (15 - step) * far
    return hops * (1 - side) + (NSLAB - hops) * side


def prepare_rows(me, slot_atom, rows_at):
    prev_start = lax.rem(me + NSLAB - 1, NSLAB) * ATOMS

    def one(k, carry):
        atom = slot_atom[k]
        rel = atom - prev_start
        rel = jnp.where(rel < 0, rel + NATOM, rel)
        rows_at[k] = jnp.where((atom < 0) | (rel >= 2 * ATOMS), 0, rel)
        return carry

    lax.fori_loop(0, SLOTS, one, 0, unroll=8)


def prepare_slots(pj, lf, lhs, bw):
    for q in range(4):
        v = pj[:, 128 * q : 128 * (q + 1)]
        lf[pl.ds(2 * q, SLOTS, stride=CH), :] = v
        lf[pl.ds(2 * q + 1, SLOTS, stride=CH), :] = pltpu.roll(v, 64, 1)
    low = iota((128, 128), 1) < 64

    def one(i, carry):
        rows = pl.ds(pl.multiple_of(i * 128, 128), 128)
        x = lf[rows, :]
        both = jnp.where(low, x, pltpu.roll(x, 64, 1))
        hi = both.astype(BF16).astype(F32)
        lo = both - hi
        lhs[rows, 0:128] = hi.astype(BF16)
        lhs[rows, 128:256] = jnp.where(low, lo, 0.0).astype(BF16)
        lf[rows, :] = both
        return carry

    lax.fori_loop(0, SLOTS * CH // 128, one, 0, unroll=2)
    keep = (iota((16, 128), 0) < 8) == (iota((16, 128), 1) < 64)

    def two(g, carry):
        for i in range(8):
            first = pl.multiple_of((g * 8 + i) * CH, CH)
            second = pl.multiple_of((HALF + g * 8 + i) * CH, CH)
            x = jnp.concatenate([lf[pl.ds(first, CH), :], lf[pl.ds(second, CH), :]], axis=0)
            x = jnp.where(keep, x, 0.0)
            hi = x.astype(BF16)
            lo = (x - hi.astype(F32)).astype(BF16)
            bw[g, 16 * i : 16 * (i + 1), 0:128] = hi
            bw[g, 16 * i : 16 * (i + 1), 128:256] = lo
        return carry

    lax.fori_loop(0, HALF // 8, two, 0)


def prepare_tables(me, atom_row, box_row, cw, sel, b4, md, start):
    slot_atom = atom_row[...]
    slot_box = box_row[...]
    live = slot_atom >= 0
    prev_start = lax.rem(me + NSLAB - 1, NSLAB) * ATOMS
    rel = slot_atom - prev_start
    rel = jnp.where(rel < 0, rel + NATOM, rel)
    rel = jnp.where(live, rel, -1)
    sel[...] = jnp.where(iota((2 * ATOMS, SLOTS), 0) == rel, 1.0, 0.0).astype(BF16)
    box = jnp.where(live, slot_box, -1)
    row = iota((TILES, HALF), 0)
    for i2 in range(2):
        part = box[:, HALF * i2 : HALF * (i2 + 1)]
        for p in range(2):
            at = (2 * i2 + p) * TILES
            b4[at : at + TILES, :] = jnp.where(2 * row + p == part, 1.0, 0.0).astype(BF16)
    offset = me * ATOMS - start
    own = jnp.where(iota((ATOMS, WIN), 1) == iota((ATOMS, WIN), 0) + offset, 1.0, 0.0)
    mixing = mm_nt(own, cw[0:72, :], lax.Precision.HIGHEST)
    count = mixing[:, 64:65]
    pair_channel = iota((ATOMS, 64), 1)
    keep = (lax.div(pair_channel, CH).astype(F32) < count) & (
        lax.rem(pair_channel, CH).astype(F32) < count
    )
    mixing = jnp.where(keep, mixing[:, 0:64], 0.0)
    pair = iota((64, CH * NB), 0)
    to = lax.div(iota((64, CH * NB), 1), NB)
    for d in range(CH):
        source = lax.rem(to + CH - d, CH)
        spread = jnp.where(pair == to * CH + source, 1.0, 0.0)
        md[d] = jnp.dot(
            mixing, spread, preferred_element_type=F32, precision=lax.Precision.HIGHEST
        )


def split_bands(xb, xs):
    low = iota((NB, 128), 1) < 64

    def one(r, carry):
        x = xb[r]
        turned = pltpu.roll(x, 64, 1)
        for p in range(2):
            both = jnp.where(low, x, turned) if p == 0 else jnp.where(low, turned, x)
            hi = both.astype(BF16).astype(F32)
            lo = both - hi
            xs[2 * r + p, :, 0:128] = jnp.where(low, hi, lo).astype(BF16)
            xs[2 * r + p, :, 128:256] = hi.astype(BF16)
        return carry

    lax.fori_loop(0, TILES, one, 0, unroll=8)


def project(slot_box, lhs, xs, pc, sel, q, between):
    def group(g):
        base = g * 8
        weights = jnp.concatenate([xs[slot_box[base + i]] for i in range(8)], axis=0)
        rows = pl.ds(pl.multiple_of(base * CH, 64), 64)
        out = mm_nt(lhs[rows, :], weights)
        for i in range(8):
            tile = out[8 * i : 8 * i + 8, 128 * (i // 4) : 128 * (i // 4 + 1)]
            if i % 4:
                tile = pltpu.roll(tile, 128 - NB * (i % 4), 1)
            pc[pl.ds(base + i, CH, stride=SLOTS), :] = tile

    def part(j, carry):
        for i in range(16):
            group(j * 16 + i)
        return carry

    lax.fori_loop(0, SLOTS // 128, part, 0)
    values = jnp.concatenate(
        [pc[SLOTS * c : SLOTS * (c + 1), 0:NB] for c in range(CH)], axis=1
    )
    hi, lo = split(values)
    for half in range(2):
        rows = slice(ATOMS * half, ATOMS * (half + 1))
        q[rows, :] = mm(sel[rows, :], hi) + mm(sel[rows, :], lo)
        if half == 0:
            between()


def couple(j, q, up, md, cf):
    rows = slice(PART * j, PART * (j + 1))
    own = slice(ATOMS + PART * j, ATOMS + PART * (j + 1))
    total = q[own, :] + up[rows, :]
    mixed = md[0, rows] * total
    for d in range(1, CH):
        mixed = mixed + md[d, rows] * pltpu.roll(total, NB * d, 1)
    cf[own, :] = mixed


def spread_rows(first, cf, k3):
    rows = slice(first, first + ATOMS)
    for c in range(CH):
        tile = cf[rows, 128 * (c // 4) : 128 * (c // 4 + 1)]
        if c % 4:
            tile = pltpu.roll(tile, 128 - NB * (c % 4), 1)
        k3[rows, c, :] = tile


def contribute(rows_at, k3, bw, cc):
    pair_of = lax.div(lax.rem(iota((NB, WIN), 1), 128), 16)

    def one(g, carry):
        parts = []
        for i in range(8):
            parts.append(k3[rows_at[g * 8 + i]])
            parts.append(k3[rows_at[HALF + g * 8 + i]])
        turned = jnp.transpose(jnp.concatenate(parts, axis=0))[0:NB, :]
        hi = turned.astype(BF16).astype(F32)
        lo = turned - hi
        both = jnp.concatenate([hi, lo], axis=1)
        rows = jnp.concatenate(
            [jnp.where(pair_of == i, both, 0.0).astype(BF16) for i in range(8)], axis=0
        )
        weights = bw[g]
        out = mm(rows, jnp.concatenate([weights, weights], axis=0))
        out = out[:, 0:128] + out[:, 128:256]
        for i in range(8):
            first = pl.multiple_of((g * 8 + i) * STEP, 8)
            cc[pl.ds(first, NB), :] = out[NB * i : NB * (i + 1), :]
        return carry

    lax.fori_loop(0, HALF // 8, one, 0, unroll=8)


def gather_boxes(n, cc, b4, y):
    low = iota((TILES, 128), 1) < 64
    hi, lo = split(cc[pl.ds(n, HALF, stride=STEP), :])
    out = mm(b4[...], jnp.concatenate([hi, lo], axis=1))
    out = out[:, 0:128] + out[:, 128:256]
    stay = jnp.where(low, out[0:32], out[96:128])
    move = jnp.where(low, out[32:64], out[64:96])
    y[n] = stay + pltpu.roll(move, 64, 1)


def kernel(
    slot_atom, slot_box, channels, bands, projectors, coupling,
    out,
    atom_row, box_row, count_row, atom_at, box_at, rows_at,
    xb, xs, pj, lf, lhs, bw, sel, b4, md, cw, pc, q, up, cf, k3, cc, y,
    in_send, in_recv, out_send, out_recv, up_send, up_recv, low_send, low_recv, load_sem, self_sem,
):
    me = lax.axis_index("slab")
    after = lax.rem(me + 1, NSLAB)
    before = lax.rem(me + NSLAB - 1, NSLAB)
    start = pl.multiple_of(jnp.minimum(lax.div(me * ATOMS, 128) * 128, NATOM - WIN), 128)

    barrier = pltpu.get_barrier_semaphore()

    def greet(i, carry):
        pl.semaphore_signal(
            barrier, inc=1, device_id={"slab": lax.rem(me + i, NSLAB)}, device_id_type=MESH
        )
        return carry

    lax.fori_loop(1, NSLAB, greet, 0)

    loads = [
        pltpu.make_async_copy(src, dst, load_sem.at[i])
        for i, (src, dst) in enumerate(
            [
                (slot_atom, atom_row),
                (slot_box, box_row),
                (channels.at[:, pl.ds(start, WIN)], count_row),
                (slot_atom.at[0], atom_at),
                (slot_box.at[0], box_at),
                (coupling.at[:, pl.ds(start, WIN)], cw.at[0:64, :]),
                (projectors, pj),
            ]
        )
    ]
    for load in loads:
        load.start()
    pl.semaphore_wait(barrier, NSLAB - 1)

    def rows_of(slab):
        return pl.ds(pl.multiple_of(slab * TILES, TILES), TILES)

    def self_in(blk):
        return pltpu.make_async_copy(
            bands.at[blk, rows_of(me), :], xb.at[blk, :, me, :], self_sem.at[blk]
        )

    def self_out(blk):
        return pltpu.make_async_copy(
            y.at[blk, me], out.at[blk, rows_of(me), :], self_sem.at[2 + blk]
        )

    def remote(src, dst, send_sem, recv_sem, peer):
        return pltpu.make_async_remote_copy(
            src, dst, send_sem, recv_sem, device_id={"slab": peer}, device_id_type=MESH
        )

    def send_in(blk, offset, batch):
        peer = lax.rem(me + offset, NSLAB)
        remote(
            bands.at[blk, rows_of(peer), :],
            xb.at[blk, :, me, :],
            in_send.at[batch],
            in_recv.at[blk],
            peer,
        ).start()

    def send_out(blk, offset):
        peer = lax.rem(me + offset, NSLAB)
        remote(
            y.at[blk, peer],
            out.at[blk, rows_of(me), :],
            out_send.at[blk],
            out_recv.at[blk],
            peer,
        ).start()

    def some(send, first, count):
        def one(i, carry):
            send(distance(first + i))
            return carry

        lax.fori_loop(0, count, one, 0)

    def bytes_of(ref, count, sem):
        part = ref.at[0:count]
        return pltpu.make_async_copy(part, part, sem)

    send_in(0, 16, 0)
    some(lambda offset: send_in(0, offset, 0), 1, EARLY - 1)
    some(lambda offset: send_in(0, offset, 1), EARLY, NSLAB - 1 - EARLY)
    self_in(0).start()
    self_in(1).start()

    def up_copy(blk, j):
        rows = slice(PART * j, PART * (j + 1))
        return remote(
            q.at[blk, rows], up.at[blk, rows], up_send.at[blk, j], up_recv.at[blk, j], before
        )

    def low_copy(blk, j):
        return remote(
            cf.at[blk, ATOMS + PART * j : ATOMS + PART * (j + 1)],
            cf.at[blk, PART * j : PART * (j + 1)],
            low_send.at[blk, j],
            low_recv.at[blk, j],
            after,
        )

    for load in loads:
        load.wait()
    prepare_slots(pj, lf, lhs, bw)
    cw[64:72, :] = jnp.broadcast_to(count_row[...].astype(F32), (8, WIN))
    prepare_tables(me, atom_row, box_row, cw, sel, b4, md, start)
    prepare_rows(me, atom_at, rows_at)
    bytes_of(xb.at[0], EARLY, in_send.at[0]).wait()
    send_in(1, 16, 2)
    some(lambda offset: send_in(1, offset, 2), 1, NSLAB - 2)

    def gather(blk, offset):
        gather_boxes(lax.rem(me + offset, NSLAB), cc, b4, y.at[blk])

    def project_block(blk):
        def send_up():
            for j in range(PARTS):
                up_copy(blk, j).start()

        self_in(blk).wait()
        bytes_of(xb.at[blk], NSLAB - 1, in_recv.at[blk]).wait()
        split_bands(xb.at[blk], xs)
        project(box_at, lhs, xs, pc, sel, q.at[blk], send_up)

    def couple_block(blk):
        for j in range(PARTS):
            up_copy(blk, j).wait_recv()
            couple(j, q.at[blk], up.at[blk], md, cf.at[blk])
            low_copy(blk, j).start()

    def contribute_block(blk):
        spread_rows(ATOMS, cf.at[blk], k3)
        for j in range(PARTS):
            low_copy(blk, j).wait_recv()
        spread_rows(0, cf.at[blk], k3)
        contribute(rows_at, k3, bw, cc)

    def return_block(blk):
        def eight(g, carry):
            for i in range(8):
                gather(blk, distance(1 + 8 * g + i))
            some(lambda offset: send_out(blk, offset), 1 + 8 * g, 8)
            return carry

        lax.fori_loop(0, 3, eight, 0)
        for i in range(25, 31):
            gather(blk, distance(i))
        gather(blk, 16)
        gather(blk, 0)
        some(lambda offset: send_out(blk, offset), 25, 6)
        send_out(blk, 16)
        self_out(blk).start()

    project_block(0)
    couple_block(0)
    project_block(1)
    contribute_block(0)
    couple_block(1)
    return_block(0)
    contribute_block(1)
    return_block(1)

    bytes_of(xb.at[0], NSLAB - 1 - EARLY, in_send.at[1]).wait()
    bytes_of(xb.at[1], NSLAB - 1, in_send.at[2]).wait()
    for blk in range(2):
        for j in range(PARTS):
            up_copy(blk, j).wait_send()
            low_copy(blk, j).wait_send()
        self_out(blk).wait()
        bytes_of(y.at[blk], NSLAB - 1, out_send.at[blk]).wait()
        bytes_of(y.at[blk], NSLAB - 1, out_recv.at[blk]).wait()


def body(bands, projectors, slot_atom, slot_box, channels, coupling):
    nblock = bands.shape[0]
    ngrid = bands.shape[-1]
    any_space = pl.BlockSpec(memory_space=pl.ANY)
    dma = pltpu.SemaphoreType.DMA
    result = pl.pallas_call(
        kernel,
        out_shape=jax.ShapeDtypeStruct((nblock, ngrid // 128, 128), F32),
        in_specs=[any_space] * 6,
        out_specs=any_space,
        scratch_shapes=[
            pltpu.VMEM((1, SLOTS), jnp.int32),
            pltpu.VMEM((1, SLOTS), jnp.int32),
            pltpu.VMEM((1, WIN), jnp.int32),
            pltpu.SMEM((SLOTS,), jnp.int32),
            pltpu.SMEM((SLOTS,), jnp.int32),
            pltpu.SMEM((SLOTS,), jnp.int32),
            pltpu.VMEM((2, TILES, NB, 128), F32),
            pltpu.VMEM((BOXES, NB, 256), BF16),
            pltpu.VMEM((SLOTS, CH * PTS), F32),
            pltpu.VMEM((SLOTS * CH, 128), F32),
            pltpu.VMEM((SLOTS * CH, 256), BF16),
            pltpu.VMEM((HALF // 8, 128, 256), BF16),
            pltpu.VMEM((2 * ATOMS, SLOTS), BF16),
            pltpu.VMEM((4 * TILES, HALF), BF16),
            pltpu.VMEM((CH, ATOMS, CH * NB), F32),
            pltpu.VMEM((72, WIN), F32),
            pltpu.VMEM((CH * SLOTS, 128), F32),
            pltpu.VMEM((2, 2 * ATOMS, CH * NB), F32),
            pltpu.VMEM((2, ATOMS, CH * NB), F32),
            pltpu.VMEM((2, 2 * ATOMS, CH * NB), F32),
            pltpu.VMEM((2 * ATOMS, CH, 128), F32),
            pltpu.VMEM((HALF * STEP, 128), F32),
            pltpu.VMEM((2, NSLAB, TILES, 128), F32),
            dma((3,)), dma((2,)), dma((2,)), dma((2,)),
            dma((2, PARTS)), dma((2, PARTS)), dma((2, PARTS)), dma((2, PARTS)),
            dma((7,)), dma((4,)),
        ],
        compiler_params=pltpu.CompilerParams(
            collective_id=0, has_side_effects=True, vmem_limit_bytes=60 * 1024 * 1024
        ),
        name="nonlocal",
    )(
        slot_atom.reshape(1, -1),
        slot_box.reshape(1, -1),
        channels.reshape(1, -1),
        bands.reshape(nblock, ngrid // 128, 128),
        projectors,
        coupling.reshape(CH * CH, -1),
    )
    return result.reshape(bands.shape)


def solution(mesh):
    in_specs = (P(None, ("band", "slab"), None), P("slab", None), P("slab"), P("slab"), P(), P())
    out_specs = P(None, ("band", "slab"), None)
    return jax.shard_map(body, mesh=mesh, in_specs=in_specs, out_specs=out_specs, check_vma=False)
```

```python
import jax
import jax.numpy as jnp
from jax import lax
from jax.experimental import pallas as pl
from jax.experimental.pallas import tpu as pltpu
from jax.sharding import PartitionSpec as P

MESH = pl.DeviceIdType.MESH
F32 = jnp.float32
BF16 = jnp.bfloat16
NSLAB = 32
PTS = 64
BOXES = 64
TILES = BOXES // 2
SLOTS = 512
HALF = SLOTS // 2
CH = 8
ATOMS = 96
NATOM = NSLAB * ATOMS
NB = 32
STEP = 40
PARTS = 3
PIECE = 16
PART = ATOMS // PARTS
WIN = 256


def split(x):
    hi = x.astype(BF16)
    lo = (x - hi.astype(F32)).astype(BF16)
    return hi, lo


def mm(a, b):
    return jnp.dot(a, b, preferred_element_type=F32)


def mm_nt(a, b, precision=None):
    return lax.dot_general(
        a, b, (((1,), (1,)), ((), ())), preferred_element_type=F32, precision=precision
    )


def iota(shape, axis):
    return lax.broadcasted_iota(jnp.int32, shape, axis)


def distance(i):
    block = lax.div(i - 1, 2)
    side = lax.rem(i - 1, 2)
    far = lax.rem(block, 2)
    step = lax.div(block, 2)
    hops = (1 + step) * (1 - far) + (15 - step) * far
    return hops * (1 - side) + (NSLAB - hops) * side


def prepare_rows(me, slot_atom, rows_at):
    prev_start = lax.rem(me + NSLAB - 1, NSLAB) * ATOMS

    def one(k, carry):
        atom = slot_atom[k]
        rel = atom - prev_start
        rel = jnp.where(rel < 0, rel + NATOM, rel)
        rows_at[k] = jnp.where((atom < 0) | (rel >= 2 * ATOMS), 0, rel)
        return carry

    lax.fori_loop(0, SLOTS, one, 0, unroll=8)


def prepare_slots(pj, lf, lhs, bw):
    for q in range(4):
        v = pj[:, 128 * q : 128 * (q + 1)]
        lf[pl.ds(2 * q, SLOTS, stride=CH), :] = v
        lf[pl.ds(2 * q + 1, SLOTS, stride=CH), :] = pltpu.roll(v, 64, 1)
    low = iota((128, 128), 1) < 64

    def one(i, carry):
        rows = pl.ds(pl.multiple_of(i * 128, 128), 128)
        x = lf[rows, :]
        both = jnp.where(low, x, pltpu.roll(x, 64, 1))
        hi = both.astype(BF16).astype(F32)
        lo = both - hi
        lhs[rows, 0:128] = hi.astype(BF16)
        lhs[rows, 128:256] = jnp.where(low, lo, 0.0).astype(BF16)
        lf[rows, :] = both
        return carry

    lax.fori_loop(0, SLOTS * CH // 128, one, 0, unroll=2)
    keep = (iota((16, 128), 0) < 8) == (iota((16, 128), 1) < 64)

    def two(g, carry):
        for i in range(8):
            first = pl.multiple_of((g * 8 + i) * CH, CH)
            second = pl.multiple_of((HALF + g * 8 + i) * CH, CH)
            x = jnp.concatenate([lf[pl.ds(first, CH), :], lf[pl.ds(second, CH), :]], axis=0)
            x = jnp.where(keep, x, 0.0)
            hi = x.astype(BF16)
            lo = (x - hi.astype(F32)).astype(BF16)
            bw[g, 16 * i : 16 * (i + 1), 0:128] = hi
            bw[g, 16 * i : 16 * (i + 1), 128:256] = lo
        return carry

    lax.fori_loop(0, HALF // 8, two, 0)


def prepare_tables(me, atom_row, box_row, cw, sel, b4, md, start):
    slot_atom = atom_row[...]
    slot_box = box_row[...]
    live = slot_atom >= 0
    prev_start = lax.rem(me + NSLAB - 1, NSLAB) * ATOMS
    rel = slot_atom - prev_start
    rel = jnp.where(rel < 0, rel + NATOM, rel)
    rel = jnp.where(live, rel, -1)
    sel[...] = jnp.where(iota((2 * ATOMS, SLOTS), 0) == rel, 1.0, 0.0).astype(BF16)
    box = jnp.where(live, slot_box, -1)
    row = iota((TILES, HALF), 0)
    for i2 in range(2):
        part = box[:, HALF * i2 : HALF * (i2 + 1)]
        for p in range(2):
            at = (2 * i2 + p) * TILES
            b4[at : at + TILES, :] = jnp.where(2 * row + p == part, 1.0, 0.0).astype(BF16)
    offset = me * ATOMS - start
    own = jnp.where(iota((ATOMS, WIN), 1) == iota((ATOMS, WIN), 0) + offset, 1.0, 0.0)
    mixing = mm_nt(own, cw[0:72, :], lax.Precision.HIGHEST)
    count = mixing[:, 64:65]
    pair_channel = iota((ATOMS, 64), 1)
    keep = (lax.div(pair_channel, CH).astype(F32) < count) & (
        lax.rem(pair_channel, CH).astype(F32) < count
    )
    mixing = jnp.where(keep, mixing[:, 0:64], 0.0)
    pair = iota((64, CH * NB), 0)
    to = lax.div(iota((64, CH * NB), 1), NB)
    for d in range(CH):
        source = lax.rem(to + CH - d, CH)
        spread = jnp.where(pair == to * CH + source, 1.0, 0.0)
        md[d] = jnp.dot(
            mixing, spread, preferred_element_type=F32, precision=lax.Precision.HIGHEST
        )


def split_bands(half, xb, xs):
    low = iota((PIECE, 128), 1) < 64
    bands = slice(PIECE * half, PIECE * (half + 1))

    def one(r, carry):
        x = xb[r, bands, :]
        turned = pltpu.roll(x, 64, 1)
        for p in range(2):
            both = jnp.where(low, x, turned) if p == 0 else jnp.where(low, turned, x)
            hi = both.astype(BF16).astype(F32)
            lo = both - hi
            xs[2 * r + p, bands, 0:128] = jnp.where(low, hi, lo).astype(BF16)
            xs[2 * r + p, bands, 128:256] = hi.astype(BF16)
        return carry

    lax.fori_loop(0, TILES, one, 0, unroll=8)


def project(half, slot_box, lhs, xs, pc):
    lanes = slice(PIECE * half, PIECE * (half + 1))

    def group(g):
        base = g * 8
        weights = jnp.concatenate([xs[slot_box[base + i]][lanes, :] for i in range(8)], axis=0)
        rows = pl.ds(pl.multiple_of(base * CH, 64), 64)
        out = mm_nt(lhs[rows, :], weights)
        for i in range(8):
            tile = out[8 * i : 8 * i + 8, :]
            if i != half:
                tile = pltpu.roll(tile, (128 + PIECE * (half - i)) % 128, 1)
            first = pl.multiple_of((base + i) * CH, CH)
            pc[pl.ds(first, CH), lanes] = tile[:, lanes]

    def part(j, carry):
        for i in range(16):
            group(j * 16 + i)
        return carry

    lax.fori_loop(0, SLOTS // 128, part, 0)


def collect(me, pc, sel, q, between):
    values = jnp.concatenate(
        [pc[pl.ds(c, SLOTS, stride=CH), :][:, 0:NB] for c in range(CH)], axis=1
    )
    hi, lo = split(values)
    shift = lax.rem(me + NSLAB - PIECE // 2, NSLAB)
    inside = lax.rem(iota((ATOMS, 128), 1), NB) >= shift
    for part in range(2):
        rows = slice(ATOMS * part, ATOMS * (part + 1))
        found = mm(sel[rows, :], hi) + mm(sel[rows, :], lo)
        for t in range(2):
            tile = found[:, 128 * t : 128 * (t + 1)]
            ahead = pltpu.roll(tile, shift, 1)
            behind = pltpu.roll(tile, lax.rem(shift + 96, 128), 1)
            q[rows, 128 * t : 128 * (t + 1)] = jnp.where(inside, ahead, behind)
        if part == 0:
            between()


def couple(j, q, up, md, cf):
    rows = slice(PART * j, PART * (j + 1))
    own = slice(ATOMS + PART * j, ATOMS + PART * (j + 1))
    total = q[own, :] + up[rows, :]
    mixed = md[0, rows] * total
    for d in range(1, CH):
        mixed = mixed + md[d, rows] * pltpu.roll(total, NB * d, 1)
    cf[own, :] = mixed


def spread_rows(first, cf, k3):
    rows = slice(first, first + ATOMS)
    for c in range(CH):
        tile = cf[rows, 128 * (c // 4) : 128 * (c // 4 + 1)]
        if c % 4:
            tile = pltpu.roll(tile, 128 - NB * (c % 4), 1)
        k3[rows, c, :] = tile


def contribute(rows_at, k3, bw, cc):
    pair_of = lax.div(lax.rem(iota((NB, WIN), 1), 128), 16)

    def one(g, carry):
        parts = []
        for i in range(8):
            parts.append(k3[rows_at[g * 8 + i]])
            parts.append(k3[rows_at[HALF + g * 8 + i]])
        turned = jnp.transpose(jnp.concatenate(parts, axis=0))[0:NB, :]
        hi = turned.astype(BF16).astype(F32)
        lo = turned - hi
        both = jnp.concatenate([hi, lo], axis=1)
        rows = jnp.concatenate(
            [jnp.where(pair_of == i, both, 0.0).astype(BF16) for i in range(8)], axis=0
        )
        weights = bw[g]
        out = mm(rows, jnp.concatenate([weights, weights], axis=0))
        out = out[:, 0:128] + out[:, 128:256]
        for i in range(8):
            first = pl.multiple_of((g * 8 + i) * STEP, 8)
            cc[pl.ds(first, NB), :] = out[NB * i : NB * (i + 1), :]
        return carry

    lax.fori_loop(0, HALF // 8, one, 0, unroll=16)


def gather_boxes(n, cc, b4, y):
    low = iota((TILES, 128), 1) < 64
    hi, lo = split(cc[pl.ds(n, HALF, stride=STEP), :])
    out = mm(b4[...], jnp.concatenate([hi, lo], axis=1))
    out = out[:, 0:128] + out[:, 128:256]
    stay = jnp.where(low, out[0:32], out[96:128])
    move = jnp.where(low, out[32:64], out[64:96])
    y[n] = stay + pltpu.roll(move, 64, 1)


def kernel(
    slot_atom, slot_box, channels, bands, projectors, coupling,
    out,
    atom_row, box_row, count_row, atom_at, box_at, rows_at,
    xb, xs, pj, lf, lhs, bw, sel, b4, md, cw, pc, q, up, cf, k3, cc, y,
    in_send, in_recv, out_send, out_recv, up_send, up_recv, low_send, low_recv, load_sem, self_sem,
):
    me = lax.axis_index("slab")
    after = lax.rem(me + 1, NSLAB)
    before = lax.rem(me + NSLAB - 1, NSLAB)
    start = pl.multiple_of(jnp.minimum(lax.div(me * ATOMS, 128) * 128, NATOM - WIN), 128)

    barrier = pltpu.get_barrier_semaphore()

    def greet(i, carry):
        pl.semaphore_signal(
            barrier, inc=1, device_id={"slab": lax.rem(me + i, NSLAB)}, device_id_type=MESH
        )
        return carry

    lax.fori_loop(1, NSLAB, greet, 0)

    loads = [
        pltpu.make_async_copy(src, dst, load_sem.at[i])
        for i, (src, dst) in enumerate(
            [
                (slot_atom, atom_row),
                (slot_box, box_row),
                (channels.at[:, pl.ds(start, WIN)], count_row),
                (slot_atom.at[0], atom_at),
                (slot_box.at[0], box_at),
                (coupling.at[:, pl.ds(start, WIN)], cw.at[0:64, :]),
                (projectors, pj),
            ]
        )
    ]
    for load in loads:
        load.start()
    pl.semaphore_wait(barrier, NSLAB - 1)

    def rows_of(slab):
        return pl.ds(pl.multiple_of(slab * TILES, TILES), TILES)

    def self_in(blk):
        return pltpu.make_async_copy(
            bands.at[blk, rows_of(me), :], xb.at[blk, :, PIECE // 2, :], self_sem.at[blk]
        )

    def self_out(blk):
        return pltpu.make_async_copy(
            y.at[blk, me], out.at[blk, rows_of(me), :], self_sem.at[2 + blk]
        )

    def remote(src, dst, send_sem, recv_sem, peer):
        return pltpu.make_async_remote_copy(
            src, dst, send_sem, recv_sem, device_id={"slab": peer}, device_id_type=MESH
        )

    def send_in(blk, half, offset):
        peer = lax.rem(me + offset, NSLAB)
        remote(
            bands.at[blk, rows_of(peer), :],
            xb.at[blk, :, lax.rem(NSLAB + PIECE // 2 - offset + NSLAB, NSLAB), :],
            in_send.at[blk, half],
            in_recv.at[blk, half],
            peer,
        ).start()

    def send_near(blk):
        def one(i, carry):
            send_in(blk, 0, i)
            send_in(blk, 0, NSLAB - i)
            return carry

        lax.fori_loop(1, 8, one, 0)
        send_in(blk, 0, 8)

    def send_far(blk):
        send_in(blk, 1, 16)
        send_in(blk, 1, 24)

        def one(i, carry):
            send_in(blk, 1, i)
            send_in(blk, 1, NSLAB - i)
            return carry

        lax.fori_loop(9, 16, one, 0)

    def send_out(blk, offset):
        peer = lax.rem(me + offset, NSLAB)
        remote(
            y.at[blk, peer],
            out.at[blk, rows_of(me), :],
            out_send.at[blk],
            out_recv.at[blk],
            peer,
        ).start()

    def some(send, first, count):
        def one(i, carry):
            send(distance(first + i))
            return carry

        lax.fori_loop(0, count, one, 0)

    def bytes_of(ref, count, sem):
        part = ref.at[0:count]
        return pltpu.make_async_copy(part, part, sem)

    send_near(0)
    send_far(0)
    self_in(0).start()
    self_in(1).start()

    def up_copy(blk, j):
        rows = slice(PART * j, PART * (j + 1))
        return remote(
            q.at[blk, rows], up.at[blk, rows], up_send.at[blk, j], up_recv.at[blk, j], before
        )

    def low_copy(blk, j):
        return remote(
            cf.at[blk, ATOMS + PART * j : ATOMS + PART * (j + 1)],
            cf.at[blk, PART * j : PART * (j + 1)],
            low_send.at[blk, j],
            low_recv.at[blk, j],
            after,
        )

    for load in loads:
        load.wait()
    prepare_slots(pj, lf, lhs, bw)
    cw[64:72, :] = jnp.broadcast_to(count_row[...].astype(F32), (8, WIN))
    prepare_tables(me, atom_row, box_row, cw, sel, b4, md, start)
    prepare_rows(me, atom_at, rows_at)
    send_near(1)
    bytes_of(xb.at[0], PIECE - 1, in_send.at[0, 0]).wait()
    send_far(1)

    def gather(blk, offset):
        gather_boxes(lax.rem(me + offset, NSLAB), cc, b4, y.at[blk])

    def project_near(blk):
        self_in(blk).wait()
        bytes_of(xb.at[blk], PIECE - 1, in_recv.at[blk, 0]).wait()
        split_bands(0, xb.at[blk], xs)
        project(0, box_at, lhs, xs, pc)

    def project_far(blk):
        def send_up():
            for j in range(PARTS):
                up_copy(blk, j).start()

        bytes_of(xb.at[blk], PIECE, in_recv.at[blk, 1]).wait()
        split_bands(1, xb.at[blk], xs)
        project(1, box_at, lhs, xs, pc)
        collect(me, pc, sel, q.at[blk], send_up)

    def couple_block(blk):
        for j in range(PARTS):
            up_copy(blk, j).wait_recv()
            couple(j, q.at[blk], up.at[blk], md, cf.at[blk])
            low_copy(blk, j).start()

    def contribute_block(blk):
        spread_rows(ATOMS, cf.at[blk], k3)
        for j in range(PARTS):
            low_copy(blk, j).wait_recv()
        spread_rows(0, cf.at[blk], k3)
        contribute(rows_at, k3, bw, cc)

    def return_block(blk):
        def eight(g, carry):
            for i in range(8):
                gather(blk, distance(1 + 8 * g + i))
            some(lambda offset: send_out(blk, offset), 1 + 8 * g, 8)
            return carry

        lax.fori_loop(0, 3, eight, 0)
        for i in range(25, 31):
            gather(blk, distance(i))
        gather(blk, 16)
        gather(blk, 0)
        some(lambda offset: send_out(blk, offset), 25, 6)
        send_out(blk, 16)
        self_out(blk).start()

    project_near(0)
    project_far(0)
    project_near(1)
    couple_block(0)
    project_far(1)
    contribute_block(0)
    couple_block(1)
    return_block(0)
    contribute_block(1)
    return_block(1)

    bytes_of(xb.at[0], PIECE, in_send.at[0, 1]).wait()
    bytes_of(xb.at[1], PIECE - 1, in_send.at[1, 0]).wait()
    bytes_of(xb.at[1], PIECE, in_send.at[1, 1]).wait()
    for blk in range(2):
        for j in range(PARTS):
            up_copy(blk, j).wait_send()
            low_copy(blk, j).wait_send()
        self_out(blk).wait()
        bytes_of(y.at[blk], NSLAB - 1, out_send.at[blk]).wait()
        bytes_of(y.at[blk], NSLAB - 1, out_recv.at[blk]).wait()


def body(bands, projectors, slot_atom, slot_box, channels, coupling):
    nblock = bands.shape[0]
    ngrid = bands.shape[-1]
    any_space = pl.BlockSpec(memory_space=pl.ANY)
    dma = pltpu.SemaphoreType.DMA
    result = pl.pallas_call(
        kernel,
        out_shape=jax.ShapeDtypeStruct((nblock, ngrid // 128, 128), F32),
        in_specs=[any_space] * 6,
        out_specs=any_space,
        scratch_shapes=[
            pltpu.VMEM((1, SLOTS), jnp.int32),
            pltpu.VMEM((1, SLOTS), jnp.int32),
            pltpu.VMEM((1, WIN), jnp.int32),
            pltpu.SMEM((SLOTS,), jnp.int32),
            pltpu.SMEM((SLOTS,), jnp.int32),
            pltpu.SMEM((SLOTS,), jnp.int32),
            pltpu.VMEM((2, TILES, NB, 128), F32),
            pltpu.VMEM((BOXES, NB, 256), BF16),
            pltpu.VMEM((SLOTS, CH * PTS), F32),
            pltpu.VMEM((SLOTS * CH, 128), F32),
            pltpu.VMEM((SLOTS * CH, 256), BF16),
            pltpu.VMEM((HALF // 8, 128, 256), BF16),
            pltpu.VMEM((2 * ATOMS, SLOTS), BF16),
            pltpu.VMEM((4 * TILES, HALF), BF16),
            pltpu.VMEM((CH, ATOMS, CH * NB), F32),
            pltpu.VMEM((72, WIN), F32),
            pltpu.VMEM((CH * SLOTS, 128), F32),
            pltpu.VMEM((2, 2 * ATOMS, CH * NB), F32),
            pltpu.VMEM((2, ATOMS, CH * NB), F32),
            pltpu.VMEM((2, 2 * ATOMS, CH * NB), F32),
            pltpu.VMEM((2 * ATOMS, CH, 128), F32),
            pltpu.VMEM((HALF * STEP, 128), F32),
            pltpu.VMEM((2, NSLAB, TILES, 128), F32),
            dma((2, 2)), dma((2, 2)), dma((2,)), dma((2,)),
            dma((2, PARTS)), dma((2, PARTS)), dma((2, PARTS)), dma((2, PARTS)),
            dma((7,)), dma((4,)),
        ],
        compiler_params=pltpu.CompilerParams(
            collective_id=0, has_side_effects=True, vmem_limit_bytes=60 * 1024 * 1024
        ),
        name="nonlocal",
    )(
        slot_atom.reshape(1, -1),
        slot_box.reshape(1, -1),
        channels.reshape(1, -1),
        bands.reshape(nblock, ngrid // 128, 128),
        projectors,
        coupling.reshape(CH * CH, -1),
    )
    return result.reshape(bands.shape)


def solution(mesh):
    in_specs = (P(None, ("band", "slab"), None), P("slab", None), P("slab"), P("slab"), P(), P())
    out_specs = P(None, ("band", "slab"), None)
    return jax.shard_map(body, mesh=mesh, in_specs=in_specs, out_specs=out_specs, check_vma=False)
```

```python
import jax
import jax.numpy as jnp
from jax import lax
from jax.experimental import pallas as pl
from jax.experimental.pallas import tpu as pltpu
from jax.sharding import PartitionSpec as P

MESH = pl.DeviceIdType.MESH
F32 = jnp.float32
BF16 = jnp.bfloat16
NSLAB = 32
PTS = 64
BOXES = 64
TILES = BOXES // 2
SLOTS = 512
HALF = SLOTS // 2
CH = 8
ATOMS = 96
NATOM = NSLAB * ATOMS
NB = 32
STEP = 40
PARTS = 2
PIECE = 16
PART = ATOMS // PARTS
WIN = 256


def split(x):
    hi = x.astype(BF16)
    lo = (x - hi.astype(F32)).astype(BF16)
    return hi, lo


def mm(a, b):
    return jnp.dot(a, b, preferred_element_type=F32)


def mm_nt(a, b, precision=None):
    return lax.dot_general(
        a, b, (((1,), (1,)), ((), ())), preferred_element_type=F32, precision=precision
    )


def iota(shape, axis):
    return lax.broadcasted_iota(jnp.int32, shape, axis)


def distance(i):
    block = lax.div(i - 1, 2)
    side = lax.rem(i - 1, 2)
    far = lax.rem(block, 2)
    step = lax.div(block, 2)
    hops = (1 + step) * (1 - far) + (15 - step) * far
    return hops * (1 - side) + (NSLAB - hops) * side


def prepare_rows(me, slot_atom, rows_at):
    prev_start = lax.rem(me + NSLAB - 1, NSLAB) * ATOMS

    def one(k, carry):
        atom = slot_atom[k]
        rel = atom - prev_start
        rel = jnp.where(rel < 0, rel + NATOM, rel)
        rows_at[k] = jnp.where((atom < 0) | (rel >= 2 * ATOMS), 0, rel)
        return carry

    lax.fori_loop(0, SLOTS, one, 0, unroll=8)


def prepare_slots(pj, lf, lhs, bw):
    for q in range(4):
        v = pj[:, 128 * q : 128 * (q + 1)]
        lf[pl.ds(2 * q, SLOTS, stride=CH), :] = v
        lf[pl.ds(2 * q + 1, SLOTS, stride=CH), :] = pltpu.roll(v, 64, 1)
    low = iota((128, 128), 1) < 64

    def one(i, carry):
        rows = pl.ds(pl.multiple_of(i * 128, 128), 128)
        x = lf[rows, :]
        both = jnp.where(low, x, pltpu.roll(x, 64, 1))
        hi = both.astype(BF16).astype(F32)
        lo = both - hi
        lhs[rows, 0:128] = hi.astype(BF16)
        lhs[rows, 128:256] = jnp.where(low, lo, 0.0).astype(BF16)
        lf[rows, :] = both
        return carry

    lax.fori_loop(0, SLOTS * CH // 128, one, 0, unroll=2)
    keep = (iota((16, 128), 0) < 8) == (iota((16, 128), 1) < 64)

    def two(g, carry):
        for i in range(8):
            first = pl.multiple_of((g * 8 + i) * CH, CH)
            second = pl.multiple_of((HALF + g * 8 + i) * CH, CH)
            x = jnp.concatenate([lf[pl.ds(first, CH), :], lf[pl.ds(second, CH), :]], axis=0)
            x = jnp.where(keep, x, 0.0)
            hi = x.astype(BF16)
            lo = (x - hi.astype(F32)).astype(BF16)
            bw[g, 16 * i : 16 * (i + 1), 0:128] = hi
            bw[g, 16 * i : 16 * (i + 1), 128:256] = lo
        return carry

    lax.fori_loop(0, HALF // 8, two, 0)


def prepare_tables(me, atom_row, box_row, cw, sel, b4, md, start):
    slot_atom = atom_row[...]
    slot_box = box_row[...]
    live = slot_atom >= 0
    prev_start = lax.rem(me + NSLAB - 1, NSLAB) * ATOMS
    rel = slot_atom - prev_start
    rel = jnp.where(rel < 0, rel + NATOM, rel)
    rel = jnp.where(live, rel, -1)
    sel[...] = jnp.where(iota((2 * ATOMS, SLOTS), 0) == rel, 1.0, 0.0).astype(BF16)
    box = jnp.where(live, slot_box, -1)
    row = iota((TILES, HALF), 0)
    for i2 in range(2):
        part = box[:, HALF * i2 : HALF * (i2 + 1)]
        for p in range(2):
            at = (2 * i2 + p) * TILES
            b4[at : at + TILES, :] = jnp.where(2 * row + p == part, 1.0, 0.0).astype(BF16)
    offset = me * ATOMS - start
    own = jnp.where(iota((ATOMS, WIN), 1) == iota((ATOMS, WIN), 0) + offset, 1.0, 0.0)
    mixing = mm_nt(own, cw[0:72, :], lax.Precision.HIGHEST)
    count = mixing[:, 64:65]
    pair_channel = iota((ATOMS, 64), 1)
    keep = (lax.div(pair_channel, CH).astype(F32) < count) & (
        lax.rem(pair_channel, CH).astype(F32) < count
    )
    mixing = jnp.where(keep, mixing[:, 0:64], 0.0)
    pair = iota((64, CH * NB), 0)
    to = lax.div(iota((64, CH * NB), 1), NB)
    for d in range(CH):
        source = lax.rem(to + CH - d, CH)
        spread = jnp.where(pair == to * CH + source, 1.0, 0.0)
        md[d] = jnp.dot(
            mixing, spread, preferred_element_type=F32, precision=lax.Precision.HIGHEST
        )


def split_bands(half, xb, xs):
    low = iota((PIECE, 128), 1) < 64
    bands = slice(PIECE * half, PIECE * (half + 1))

    def one(r, carry):
        x = xb[r, bands, :]
        turned = pltpu.roll(x, 64, 1)
        for p in range(2):
            both = jnp.where(low, x, turned) if p == 0 else jnp.where(low, turned, x)
            hi = both.astype(BF16).astype(F32)
            lo = both - hi
            xs[2 * r + p, bands, 0:128] = jnp.where(low, hi, lo).astype(BF16)
            xs[2 * r + p, bands, 128:256] = hi.astype(BF16)
        return carry

    lax.fori_loop(0, TILES, one, 0, unroll=8)


def project(half, slot_box, lhs, xs, pc):
    lanes = slice(PIECE * half, PIECE * (half + 1))

    def group(g):
        base = g * 8
        weights = jnp.concatenate([xs[slot_box[base + i]][lanes, :] for i in range(8)], axis=0)
        rows = pl.ds(pl.multiple_of(base * CH, 64), 64)
        out = mm_nt(lhs[rows, :], weights)
        for i in range(8):
            tile = out[8 * i : 8 * i + 8, :]
            if i != half:
                tile = pltpu.roll(tile, (128 + PIECE * (half - i)) % 128, 1)
            first = pl.multiple_of((base + i) * CH, CH)
            pc[pl.ds(first, CH), lanes] = tile[:, lanes]

    def part(j, carry):
        for i in range(16):
            group(j * 16 + i)
        return carry

    lax.fori_loop(0, SLOTS // 128, part, 0)


def collect(me, pc, sel, q, between):
    values = jnp.concatenate(
        [pc[pl.ds(c, SLOTS, stride=CH), :][:, 0:NB] for c in range(CH)], axis=1
    )
    hi, lo = split(values)
    shift = lax.rem(me + NSLAB - PIECE // 2, NSLAB)
    inside = lax.rem(iota((ATOMS, 128), 1), NB) >= shift
    for part in range(2):
        rows = slice(ATOMS * part, ATOMS * (part + 1))
        found = mm(sel[rows, :], hi) + mm(sel[rows, :], lo)
        for t in range(2):
            tile = found[:, 128 * t : 128 * (t + 1)]
            ahead = pltpu.roll(tile, shift, 1)
            behind = pltpu.roll(tile, lax.rem(shift + 96, 128), 1)
            q[rows, 128 * t : 128 * (t + 1)] = jnp.where(inside, ahead, behind)
        if part == 0:
            between()


def couple(j, q, up, md, cf):
    rows = slice(PART * j, PART * (j + 1))
    own = slice(ATOMS + PART * j, ATOMS + PART * (j + 1))
    total = q[own, :] + up[rows, :]
    mixed = md[0, rows] * total
    for d in range(1, CH):
        mixed = mixed + md[d, rows] * pltpu.roll(total, NB * d, 1)
    cf[own, :] = mixed


def spread_rows(first, cf, k3):
    rows = slice(first, first + ATOMS)
    for c in range(CH):
        tile = cf[rows, 128 * (c // 4) : 128 * (c // 4 + 1)]
        if c % 4:
            tile = pltpu.roll(tile, 128 - NB * (c % 4), 1)
        k3[rows, c, :] = tile


def contribute(rows_at, k3, bw, cc):
    pair_of = lax.div(lax.rem(iota((NB, WIN), 1), 128), 16)

    def one(g, carry):
        parts = []
        for i in range(8):
            parts.append(k3[rows_at[g * 8 + i]])
            parts.append(k3[rows_at[HALF + g * 8 + i]])
        turned = jnp.transpose(jnp.concatenate(parts, axis=0))[0:NB, :]
        hi = turned.astype(BF16).astype(F32)
        lo = turned - hi
        both = jnp.concatenate([hi, lo], axis=1)
        rows = jnp.concatenate(
            [jnp.where(pair_of == i, both, 0.0).astype(BF16) for i in range(8)], axis=0
        )
        weights = bw[g]
        out = mm(rows, jnp.concatenate([weights, weights], axis=0))
        out = out[:, 0:128] + out[:, 128:256]
        for i in range(8):
            first = pl.multiple_of((g * 8 + i) * STEP, 8)
            cc[pl.ds(first, NB), :] = out[NB * i : NB * (i + 1), :]
        return carry

    lax.fori_loop(0, HALF // 8, one, 0, unroll=16)


def gather_boxes(n, cc, b4, y):
    low = iota((TILES, 128), 1) < 64
    hi, lo = split(cc[pl.ds(n, HALF, stride=STEP), :])
    out = mm(b4[...], jnp.concatenate([hi, lo], axis=1))
    out = out[:, 0:128] + out[:, 128:256]
    stay = jnp.where(low, out[0:32], out[96:128])
    move = jnp.where(low, out[32:64], out[64:96])
    y[n] = stay + pltpu.roll(move, 64, 1)


def kernel(
    slot_atom, slot_box, channels, bands, projectors, coupling,
    out,
    atom_row, box_row, count_row, atom_at, box_at, rows_at,
    xb, xs, pj, lf, lhs, bw, sel, b4, md, cw, pc, q, up, cf, k3, cc, y,
    in_send, in_recv, out_send, out_recv, up_send, up_recv, low_send, low_recv, load_sem, self_sem,
):
    me = lax.axis_index("slab")
    after = lax.rem(me + 1, NSLAB)
    before = lax.rem(me + NSLAB - 1, NSLAB)
    start = pl.multiple_of(jnp.minimum(lax.div(me * ATOMS, 128) * 128, NATOM - WIN), 128)

    barrier = pltpu.get_barrier_semaphore()

    def greet(i, carry):
        pl.semaphore_signal(
            barrier, inc=1, device_id={"slab": lax.rem(me + i, NSLAB)}, device_id_type=MESH
        )
        return carry

    lax.fori_loop(1, NSLAB, greet, 0)

    loads = [
        pltpu.make_async_copy(src, dst, load_sem.at[i])
        for i, (src, dst) in enumerate(
            [
                (slot_atom, atom_row),
                (slot_box, box_row),
                (channels.at[:, pl.ds(start, WIN)], count_row),
                (slot_atom.at[0], atom_at),
                (slot_box.at[0], box_at),
                (coupling.at[:, pl.ds(start, WIN)], cw.at[0:64, :]),
                (projectors, pj),
            ]
        )
    ]
    for load in loads:
        load.start()
    pl.semaphore_wait(barrier, NSLAB - 1)

    def rows_of(slab):
        return pl.ds(pl.multiple_of(slab * TILES, TILES), TILES)

    def self_in(blk):
        return pltpu.make_async_copy(
            bands.at[blk, rows_of(me), :], xb.at[blk, :, PIECE // 2, :], self_sem.at[blk]
        )

    def self_out(blk):
        return pltpu.make_async_copy(
            y.at[blk, me], out.at[blk, rows_of(me), :], self_sem.at[2 + blk]
        )

    def remote(src, dst, send_sem, recv_sem, peer):
        return pltpu.make_async_remote_copy(
            src, dst, send_sem, recv_sem, device_id={"slab": peer}, device_id_type=MESH
        )

    def send_in(blk, half, offset):
        peer = lax.rem(me + offset, NSLAB)
        remote(
            bands.at[blk, rows_of(peer), :],
            xb.at[blk, :, lax.rem(NSLAB + PIECE // 2 - offset + NSLAB, NSLAB), :],
            in_send.at[blk, half],
            in_recv.at[blk, half],
            peer,
        ).start()

    def send_near(blk):
        def one(i, carry):
            send_in(blk, 0, i)
            send_in(blk, 0, NSLAB - i)
            return carry

        lax.fori_loop(1, 8, one, 0)
        send_in(blk, 0, 8)

    def send_far(blk):
        send_in(blk, 1, 16)
        send_in(blk, 1, 24)

        def one(i, carry):
            send_in(blk, 1, i)
            send_in(blk, 1, NSLAB - i)
            return carry

        lax.fori_loop(9, 16, one, 0)

    def send_out(blk, offset):
        peer = lax.rem(me + offset, NSLAB)
        remote(
            y.at[blk, peer],
            out.at[blk, rows_of(me), :],
            out_send.at[blk],
            out_recv.at[blk],
            peer,
        ).start()

    def some(send, first, count):
        def one(i, carry):
            send(distance(first + i))
            return carry

        lax.fori_loop(0, count, one, 0)

    def bytes_of(ref, count, sem):
        part = ref.at[0:count]
        return pltpu.make_async_copy(part, part, sem)

    send_near(0)
    send_far(0)
    self_in(0).start()
    self_in(1).start()

    def up_copy(blk, j):
        rows = slice(PART * j, PART * (j + 1))
        return remote(
            q.at[blk, rows], up.at[blk, rows], up_send.at[blk, j], up_recv.at[blk, j], before
        )

    def low_copy(blk, j):
        return remote(
            cf.at[blk, ATOMS + PART * j : ATOMS + PART * (j + 1)],
            cf.at[blk, PART * j : PART * (j + 1)],
            low_send.at[blk, j],
            low_recv.at[blk, j],
            after,
        )

    for load in loads:
        load.wait()
    prepare_slots(pj, lf, lhs, bw)
    cw[64:72, :] = jnp.broadcast_to(count_row[...].astype(F32), (8, WIN))
    prepare_tables(me, atom_row, box_row, cw, sel, b4, md, start)
    prepare_rows(me, atom_at, rows_at)
    send_near(1)
    bytes_of(xb.at[0], PIECE - 1, in_send.at[0, 0]).wait()
    send_far(1)

    def gather(blk, offset):
        gather_boxes(lax.rem(me + offset, NSLAB), cc, b4, y.at[blk])

    def project_near(blk):
        self_in(blk).wait()
        bytes_of(xb.at[blk], PIECE - 1, in_recv.at[blk, 0]).wait()
        split_bands(0, xb.at[blk], xs)
        project(0, box_at, lhs, xs, pc)

    def project_far(blk):
        def send_up():
            for j in range(PARTS):
                up_copy(blk, j).start()

        bytes_of(xb.at[blk], PIECE, in_recv.at[blk, 1]).wait()
        split_bands(1, xb.at[blk], xs)
        project(1, box_at, lhs, xs, pc)
        collect(me, pc, sel, q.at[blk], send_up)

    def couple_block(blk):
        for j in range(PARTS):
            up_copy(blk, j).wait_recv()
            couple(j, q.at[blk], up.at[blk], md, cf.at[blk])
            low_copy(blk, j).start()

    def contribute_block(blk):
        spread_rows(ATOMS, cf.at[blk], k3)
        for j in range(PARTS):
            low_copy(blk, j).wait_recv()
        spread_rows(0, cf.at[blk], k3)
        contribute(rows_at, k3, bw, cc)

    def return_block(blk):
        def eight(g, carry):
            for j in range(2):
                for i in range(4):
                    gather(blk, distance(1 + 8 * g + 4 * j + i))
                some(lambda offset: send_out(blk, offset), 1 + 8 * g + 4 * j, 4)
            return carry

        lax.fori_loop(0, 3, eight, 0)
        for i in range(25, 31):
            gather(blk, distance(i))
        gather(blk, 16)
        gather(blk, 0)
        some(lambda offset: send_out(blk, offset), 25, 6)
        send_out(blk, 16)
        self_out(blk).start()

    project_near(0)
    project_far(0)
    project_near(1)
    couple_block(0)
    project_far(1)
    contribute_block(0)
    couple_block(1)
    return_block(0)
    contribute_block(1)
    return_block(1)

    bytes_of(xb.at[0], PIECE, in_send.at[0, 1]).wait()
    bytes_of(xb.at[1], PIECE - 1, in_send.at[1, 0]).wait()
    bytes_of(xb.at[1], PIECE, in_send.at[1, 1]).wait()
    for blk in range(2):
        for j in range(PARTS):
            up_copy(blk, j).wait_send()
            low_copy(blk, j).wait_send()
        self_out(blk).wait()
        bytes_of(y.at[blk], NSLAB - 1, out_send.at[blk]).wait()
        bytes_of(y.at[blk], NSLAB - 1, out_recv.at[blk]).wait()


def body(bands, projectors, slot_atom, slot_box, channels, coupling):
    nblock = bands.shape[0]
    ngrid = bands.shape[-1]
    any_space = pl.BlockSpec(memory_space=pl.ANY)
    dma = pltpu.SemaphoreType.DMA
    result = pl.pallas_call(
        kernel,
        out_shape=jax.ShapeDtypeStruct((nblock, ngrid // 128, 128), F32),
        in_specs=[any_space] * 6,
        out_specs=any_space,
        scratch_shapes=[
            pltpu.VMEM((1, SLOTS), jnp.int32),
            pltpu.VMEM((1, SLOTS), jnp.int32),
            pltpu.VMEM((1, WIN), jnp.int32),
            pltpu.SMEM((SLOTS,), jnp.int32),
            pltpu.SMEM((SLOTS,), jnp.int32),
            pltpu.SMEM((SLOTS,), jnp.int32),
            pltpu.VMEM((2, TILES, NB, 128), F32),
            pltpu.VMEM((BOXES, NB, 256), BF16),
            pltpu.VMEM((SLOTS, CH * PTS), F32),
            pltpu.VMEM((SLOTS * CH, 128), F32),
            pltpu.VMEM((SLOTS * CH, 256), BF16),
            pltpu.VMEM((HALF // 8, 128, 256), BF16),
            pltpu.VMEM((2 * ATOMS, SLOTS), BF16),
            pltpu.VMEM((4 * TILES, HALF), BF16),
            pltpu.VMEM((CH, ATOMS, CH * NB), F32),
            pltpu.VMEM((72, WIN), F32),
            pltpu.VMEM((CH * SLOTS, 128), F32),
            pltpu.VMEM((2, 2 * ATOMS, CH * NB), F32),
            pltpu.VMEM((2, ATOMS, CH * NB), F32),
            pltpu.VMEM((2, 2 * ATOMS, CH * NB), F32),
            pltpu.VMEM((2 * ATOMS, CH, 128), F32),
            pltpu.VMEM((HALF * STEP, 128), F32),
            pltpu.VMEM((2, NSLAB, TILES, 128), F32),
            dma((2, 2)), dma((2, 2)), dma((2,)), dma((2,)),
            dma((2, PARTS)), dma((2, PARTS)), dma((2, PARTS)), dma((2, PARTS)),
            dma((7,)), dma((4,)),
        ],
        compiler_params=pltpu.CompilerParams(
            collective_id=0, has_side_effects=True, vmem_limit_bytes=60 * 1024 * 1024
        ),
        name="nonlocal",
    )(
        slot_atom.reshape(1, -1),
        slot_box.reshape(1, -1),
        channels.reshape(1, -1),
        bands.reshape(nblock, ngrid // 128, 128),
        projectors,
        coupling.reshape(CH * CH, -1),
    )
    return result.reshape(bands.shape)


def solution(mesh):
    in_specs = (P(None, ("band", "slab"), None), P("slab", None), P("slab"), P("slab"), P(), P())
    out_specs = P(None, ("band", "slab"), None)
    return jax.shard_map(body, mesh=mesh, in_specs=in_specs, out_specs=out_specs, check_vma=False)
```
